128 devices in a mesh: row: 8 (over y, core), col: 16 (over x, z).
Axes of the slice: x: 4, y: 4, z: 4, core: 2. Of those that a mesh axis runs over, the one named last changes fastest.
Arguments:
- tokens: bfloat16 [12288, 2048], P('col', 'row'), may hold values from -6 to 6
- teacher: bfloat16 [12288, 2048], P('col', 'row'), may hold values from -6 to 6
- gate_weight: bfloat16 [2048, 10240], P('col', 'row'), may hold values from -0.25 to 0.25
- up_weight: bfloat16 [2048, 10240], P('col', 'row'), may hold values from -0.25 to 0.25
- down_weight: bfloat16 [10240, 2048], P('row', 'col'), may hold values from -0.109375 to 0.109375
- gate_mask: int32 [16, 80], P(None, 'row'), may hold values from 0 to 1, as said below
- up_mask: int32 [16, 80], P(None, 'row'), may hold values from 0 to 1, as said below
- down_mask: int32 [80, 16], P('row'), may hold values from 0 to 1, as said below
Outputs:
- student: bfloat16 [12288, 2048], P('col', 'row')
- grad_gate: float32 [2048, 10240], P('col', 'row')
- grad_up: float32 [2048, 10240], P('col', 'row')
- grad_down: float32 [10240, 2048], P('row', 'col')
The draws below stay inside these ranges and needn't reach their ends.
Inputs may be any that keep to these rules, and one draw needn't show every extreme that they name: `gate_mask`: 1 marks a live block. The weight tile of one device, 1 x 10 blocks, holds between 2 and 4 live blocks, and some tile exactly 4. `up_mask`: 1 marks a live block. The weight tile of one device, 1 x 10 blocks, holds between 2 and 4 live blocks, and some tile exactly 4. `down_mask`: 1 marks a live block. The weight tile of one device, 10 x 1 block, holds between 2 and 4 live blocks, and some tile exactly 4.
All inputs are finite; a program needn't handle non-finite values.
Results may differ from the reference program's by a relative error of at most 0.019.
Values may be sent and summed in bfloat16 or wider, within the bound.
No kernel may reach another device: no remote copies, remote signals or barrier semaphores. Data moves between devices by JAX's collectives and lax.ppermute only.
A program may use at most 320 MiB of HBM per device.

```python
import math
import jax
import jax.numpy as jnp
from jax import lax

D = 2048
FF = 10240
BLOCK = 128
TOKENS = 12288
D_BLOCKS = 16
F_BLOCKS = 80
TILE_ROWS = 1
TILE_COLS = 10
LIVE_MOST = 4


def tile_pattern(key, grid_rows, grid_cols, block_rows, block_cols, most):
    first_key, second_key, third_key = jax.random.split(key, 3)
    tile_count = grid_rows * grid_cols
    tile_blocks = block_rows * block_cols
    scores = jax.random.randint(first_key, (tile_count, tile_blocks), 0, 1 << 20) * tile_blocks + jnp.arange(tile_blocks, dtype=jnp.int32)[None, :]
    ranks = jnp.argsort(jnp.argsort(scores, axis=1), axis=1).astype(jnp.int32)
    counts = jax.random.randint(second_key, (tile_count,), most // 2, most + 1)
    full_tile = jax.random.randint(third_key, (), 0, tile_count)
    counts = jnp.where(jnp.arange(tile_count, dtype=jnp.int32) == full_tile, most, counts)
    live = (ranks < counts[:, None]).astype(jnp.int32)
    live = live.reshape(grid_rows, grid_cols, block_rows, block_cols).transpose(0, 2, 1, 3)
    return live.reshape(grid_rows * block_rows, grid_cols * block_cols)


def draw_gate_mask(key, part):
    return tile_pattern(jax.random.fold_in(key, 11), D_BLOCKS // TILE_ROWS, F_BLOCKS // TILE_COLS, TILE_ROWS, TILE_COLS, LIVE_MOST)


def draw_up_mask(key, part):
    return tile_pattern(jax.random.fold_in(key, 12), D_BLOCKS // TILE_ROWS, F_BLOCKS // TILE_COLS, TILE_ROWS, TILE_COLS, LIVE_MOST)


def draw_down_mask(key, part):
    return tile_pattern(jax.random.fold_in(key, 13), F_BLOCKS // TILE_COLS, D_BLOCKS // TILE_ROWS, TILE_COLS, TILE_ROWS, LIVE_MOST)


def with_spikes(drawn, rng, source, target, blocks, factor):
    def block_of(dim):
        return (jnp.arange(drawn.shape[dim]) // (drawn.shape[dim] // blocks)).reshape((-1,) + (1,) * (drawn.ndim - 1 - dim))

    one_side = jax.random.permutation(rng, blocks)[block_of(target)]
    second = (block_of(target) + blocks // 2) % blocks
    return jnp.where((block_of(source) == one_side) | (block_of(source) == second), factor * drawn, drawn)


def shard_levels(key, shape, cuts, least, largest):
    def one(position, blocks):
        heights = jax.random.uniform(jax.random.fold_in(jax.random.fold_in(key, 6), position), (blocks,), jnp.float32, least / len(cuts), largest / len(cuts))
        return jnp.repeat(jnp.exp(heights), shape[position] // blocks).reshape((-1,) + (1,) * (len(shape) - position - 1))

    loudness = one(*cuts[0])
    for cut in cuts[1:]:
        loudness = loudness * one(*cut)
    return loudness


def centred(stream_key, extent, deviation, most, cuts=(), held_as=jnp.bfloat16):
    array = jax.random.normal(stream_key, extent, jnp.float32) * deviation
    if len(cuts) > 0:
        array = shard_levels(stream_key, extent, cuts, -0.22, 0.18) * array
    return jnp.clip(array, min=-most, max=most).astype(held_as)


def gaussian_with(stream_key, dims, spread, reach, cuts, heavy, held_as=jnp.bfloat16):
    drawn = spread * jax.random.normal(stream_key, dims, jnp.float32)
    if cuts:
        drawn = drawn * shard_levels(stream_key, dims, cuts, -0.22, 0.18)
    return jnp.clip(with_spikes(drawn, jax.random.fold_in(stream_key, 3), *heavy), -reach, reach).astype(held_as)


def setup_inputs(seed: int = 0) -> dict:
    keys = jax.random.split(jax.random.key(seed), 9)
    tokens = gaussian_with(keys[0], (TOKENS, D), 1.0, 6.0, ((0, 16), (1, 8)), (0, 1, 16, 2.0))
    teacher = centred(keys[1], (TOKENS, D), 1.0, 6.0, ((0, 16), (1, 8)))
    gate_weight = centred(keys[2], (D, FF), (D * 3 // 10) ** -0.5, 0.25, ((0, 16), (1, 8)))
    up_weight = centred(keys[3], (D, FF), (D * 3 // 10) ** -0.5, 0.25, ((0, 16), (1, 8)))
    down_weight = centred(keys[4], (FF, D), (FF * 3 // 10) ** -0.5, 0.109375, ((0, 8), (1, 16)))
    gate_mask = draw_gate_mask(jax.random.fold_in(keys[8], 71), 0)
    up_mask = draw_up_mask(jax.random.fold_in(keys[8], 71), 0)
    down_mask = draw_down_mask(jax.random.fold_in(keys[8], 71), 0)
    return {"tokens": tokens, "teacher": teacher, "gate_weight": gate_weight, "up_weight": up_weight, "down_weight": down_weight, "gate_mask": gate_mask, "up_mask": up_mask, "down_mask": down_mask}


EPSILON = 1e-06

def spread_mask(mask):
    return jnp.repeat(jnp.repeat(mask, BLOCK, axis=0), BLOCK, axis=1)

def masked(weight, mask):
    return jnp.where(spread_mask(mask) == 1, weight, jnp.zeros_like(weight))

def reference(tokens, teacher, gate_weight, up_weight, down_weight, gate_mask, up_mask, down_mask):
    w_gate = masked(gate_weight, gate_mask)
    w_up = masked(up_weight, up_mask)
    w_down = masked(down_weight, down_mask)
    tokens_f32 = tokens.astype(jnp.float32)
    mean_square = lax.optimization_barrier(jnp.mean(tokens_f32 * tokens_f32, axis=1, keepdims=True))
    normed = (tokens_f32 * lax.rsqrt(mean_square + EPSILON)).astype(jnp.bfloat16)
    gate = jnp.dot(normed, w_gate, preferred_element_type=jnp.float32)
    upward = jnp.dot(normed, w_up, preferred_element_type=jnp.float32)
    sigmoid_gate = jax.nn.sigmoid(gate)
    silu_gate = gate * sigmoid_gate
    hidden = (silu_gate * upward).astype(jnp.bfloat16)
    branch = jnp.dot(hidden, w_down, preferred_element_type=jnp.float32)
    student = (tokens_f32 + branch).astype(jnp.bfloat16)
    grad_scale = 1.0 / math.sqrt(TOKENS)
    grad_out = ((student.astype(jnp.float32) - teacher.astype(jnp.float32)) * grad_scale).astype(jnp.bfloat16)
    grad_hidden = jnp.dot(grad_out, w_down.T, preferred_element_type=jnp.float32)
    grad_gate_act = (grad_hidden * upward * (sigmoid_gate * (1.0 + gate * (1.0 - sigmoid_gate)))).astype(jnp.bfloat16)
    grad_up_act = (grad_hidden * silu_gate).astype(jnp.bfloat16)
    grad_gate = jnp.dot(normed.T, grad_gate_act, preferred_element_type=jnp.float32) * spread_mask(gate_mask).astype(jnp.float32)
    grad_up = jnp.dot(normed.T, grad_up_act, preferred_element_type=jnp.float32) * spread_mask(up_mask).astype(jnp.float32)
    grad_down = jnp.dot(hidden.T, grad_out, preferred_element_type=jnp.float32) * spread_mask(down_mask).astype(jnp.float32)
    return (student, grad_gate, grad_up, grad_down)
```

```python
import functools
import math

import jax
import jax.numpy as jnp
from jax import lax
from jax.experimental import pallas as pl
from jax.experimental.pallas import tpu as pltpu
from jax.sharding import PartitionSpec as P

BLOCK = 128
EPSILON = 1e-06
SLOTS = 4
SIDE = 4
BF16 = jnp.bfloat16
F32 = jnp.float32


def _row_perm(dy, flip):
    return [
        (y * 2 + c, ((y + dy) % SIDE) * 2 + (c ^ flip)) for y in range(SIDE) for c in range(2)
    ]


def y_shift(v, d):
    return lax.ppermute(v, "row", _row_perm(d, 0))


def core_swap(v):
    return lax.ppermute(v, "row", _row_perm(0, 1))


def _plane_shift(stage):
    def shift(v, d):
        perm = []
        for y in range(SIDE):
            for c in range(2):
                for x in range(SIDE):
                    for z in range(SIDE):
                        if (c == 0) == (stage == 0):
                            tx, tz = (x + d) % SIDE, z
                        else:
                            tx, tz = x, (z + d) % SIDE
                        r = (y * 2 + c) * 16
                        perm.append((r + x * 4 + z, r + tx * 4 + tz))
        return lax.ppermute(v, ("row", "col"), perm)

    return shift


def ring_gather(v, shift):
    half = v.shape[0] // 2
    before = shift(v, 1)
    after = shift(v, -1)
    low = shift(before[:half], 1)
    high = shift(after[half:], -1)
    return v, after, low, high, before


def _add(a, b):
    return (a.astype(F32) + b.astype(F32)).astype(a.dtype)


def _params(mib):
    return pltpu.CompilerParams(vmem_limit_bytes=mib << 20)


def _smem():
    return pl.BlockSpec(memory_space=pltpu.SMEM)


def _vmem():
    return pl.BlockSpec(memory_space=pltpu.VMEM)


def pack_kernel(order_ref, pos_ref, gate_ref, up_ref, down_ref, keep_ref, give_ref, down_out):
    core = pos_ref[3]
    for w, src in enumerate((gate_ref, up_ref)):
        for s in range(2):
            for out, first in ((keep_ref, 2 * core), (give_ref, 2 * (1 - core))):
                j = order_ref[w * SLOTS + first + s]
                at = pl.multiple_of(jnp.maximum(j, 0) * BLOCK, BLOCK)
                block = src[:, pl.ds(at, BLOCK)]
                out[w * 2 + s] = jnp.where(j >= 0, block, jnp.zeros_like(block))
    for s in range(SLOTS):
        j = order_ref[2 * SLOTS + s]
        at = pl.multiple_of(jnp.maximum(j, 0) * BLOCK, BLOCK)
        block = down_ref[pl.ds(at, BLOCK), :]
        down_out[s] = jnp.where(j >= 0, block, jnp.zeros_like(block))


def norm_kernel(pos_ref, own, after, across, before, sw_near, sw_across, out_ref):
    y, core = pos_ref[2], pos_ref[3]
    pieces = []
    for dy, ref in enumerate((own, after, across, before)):
        pieces.append((dy, core, ref[...]))
    for n, dy in enumerate((0, 1, 3)):
        pieces.append((dy, 1 - core, sw_near[n]))
    pieces.append((2, 1 - core, sw_across[...]))
    total = None
    width = 0
    for _, _, v in pieces:
        f = v.astype(F32)
        part = jnp.sum(f * f, axis=1, keepdims=True)
        total = part if total is None else total + part
        width += v.shape[1]
    scale = lax.rsqrt(total * (1.0 / width) + EPSILON)
    for dy, c, v in pieces:
        r = lax.rem(y + dy, SIDE) * 2 + c
        at = pl.multiple_of(r * v.shape[1], v.shape[1])
        out_ref[:, pl.ds(at, v.shape[1])] = (v.astype(F32) * scale).astype(BF16)


def _piece_index(pos_ref, first, second, core):
    x, z = pos_ref[0], pos_ref[1]
    dx = jnp.where(core == 0, first, second)
    dz = jnp.where(core == 0, second, first)
    return lax.rem(x + dx, SIDE) * SIDE + lax.rem(z + dz, SIDE)


def gate_up_kernel(order_ref, pos_ref, x_ref, *refs):
    packed = (refs[0:6], refs[6:12])
    hidden_ref, slope_ref, silu_ref, dense_gate, dense_up = refs[12:]
    core = pos_ref[3]

    @pl.when(pl.program_id(0) == 0)
    def _():
        for w, dense in enumerate((dense_gate, dense_up)):
            own, after, low, before, sw_near, sw_across = packed[w]
            dense[...] = jnp.zeros_like(dense)
            for mine in (True, False):
                holder = core if mine else 1 - core
                for second in range(SIDE):
                    for first in range(SIDE):
                        k = _piece_index(pos_ref, first, second, holder)
                        row = pl.multiple_of(k * BLOCK, BLOCK)
                        for s in range(2):
                            if mine:
                                if second == 2:
                                    block = low[first, s]
                                else:
                                    block = {0: own, 1: after, 3: before}[second][0, first, s]
                            elif second == 2:
                                block = sw_across[first, s]
                            else:
                                block = sw_near[{0: 0, 1: 1, 3: 2}[second], first, s]
                            j = order_ref[w * 64 + k * SLOTS + 2 * holder + s]

                            @pl.when(j >= 0)
                            def _(dense=dense, row=row, j=j, block=block):
                                col = pl.multiple_of(j * BLOCK, BLOCK)
                                dense[pl.ds(row, BLOCK), pl.ds(col, BLOCK)] = block

    tile = hidden_ref.shape[1]
    at = pl.multiple_of(pl.program_id(0) * tile, tile)
    x = x_ref[...]
    gate = jnp.dot(x, dense_gate[:, pl.ds(at, tile)], preferred_element_type=F32)
    up = jnp.dot(x, dense_up[:, pl.ds(at, tile)], preferred_element_type=F32)
    sig = jax.nn.sigmoid(gate)
    silu = gate * sig
    hidden_ref[...] = (silu * up).astype(BF16)
    slope_ref[...] = up * (sig * (1.0 + gate * (1.0 - sig)))
    silu_ref[...] = silu


def _dense_down(order_ref, packed, dense):
    dense[...] = jnp.zeros_like(dense)
    for k in range(16):
        for s in range(SLOTS):
            j = order_ref[128 + k * SLOTS + s]

            @pl.when(j >= 0)
            def _(k=k, s=s, j=j):
                row = pl.multiple_of(j * BLOCK, BLOCK)
                dense[pl.ds(row, BLOCK), k * BLOCK : (k + 1) * BLOCK] = packed[k * SLOTS + s]


def down_kernel(order_ref, pos_ref, hidden_ref, packed, give_ref, keep_ref, dense):
    i = pl.program_id(0)

    @pl.when(i == 0)
    def _():
        _dense_down(order_ref, packed, dense)

    y, core = pos_ref[2], pos_ref[3]
    tile = keep_ref.shape[2]

    def part(dy, c):
        at = pl.multiple_of((lax.rem(y + dy, SIDE) * 2 + c) * tile, tile)
        return jnp.dot(
            hidden_ref[...], dense[:, pl.ds(at, tile)], preferred_element_type=F32
        ).astype(BF16)

    @pl.when(i < SIDE)
    def _():
        give_ref[0] = part(i, 1 - core)

    @pl.when(i >= SIDE)
    def _():
        keep_ref[0] = part(i - SIDE, core)


def down_grad_kernel(
    slot_ref, pos_ref, hidden_t, own, after, across, before, sw_near, sw_across, out_ref
):
    y, core = pos_ref[2], pos_ref[3]
    out_ref[...] = jnp.zeros_like(out_ref)
    for n in range(8):
        dy = n % SIDE
        c = core if n < SIDE else 1 - core
        if n < SIDE:
            piece = (own, after, across, before)[dy][...]
        elif dy == 2:
            piece = sw_across[...]
        else:
            piece = sw_near[{0: 0, 1: 1, 3: 2}[dy]]
        r = lax.rem(y + dy, SIDE) * 2 + c
        term = jnp.dot(hidden_t[...], piece, preferred_element_type=F32).astype(BF16)
        for half in range(2):
            k = r * 2 + half
            for j in range(10):
                slot = slot_ref[320 + k * 10 + j]

                @pl.when(slot >= 0)
                def _(k=k, j=j, half=half, slot=slot, term=term):
                    out_ref[k * SLOTS + slot] = term[
                        j * BLOCK : (j + 1) * BLOCK, half * BLOCK : (half + 1) * BLOCK
                    ]


def act_grad_kernel(
    order_ref,
    slot_ref,
    pos_ref,
    own,
    after,
    across,
    before,
    sw_near,
    sw_across,
    packed,
    slope_ref,
    silu_ref,
    normed_t,
    keep_ref,
    give_ref,
    dense,
    grad,
    term_ref,
):
    i = pl.program_id(0)
    x, z, y, core = pos_ref[0], pos_ref[1], pos_ref[2], pos_ref[3]

    @pl.when(i == 0)
    def _():
        keep_ref[...] = jnp.zeros_like(keep_ref)
        give_ref[...] = jnp.zeros_like(give_ref)
        _dense_down(order_ref, packed, dense)
        for n in range(8):
            dy = n % SIDE
            c = core if n < SIDE else 1 - core
            if n < SIDE:
                piece = (own, after, across, before)[dy][...]
            elif dy == 2:
                piece = sw_across[...]
            else:
                piece = sw_near[{0: 0, 1: 1, 3: 2}[dy]]
            width = piece.shape[1]
            at = pl.multiple_of((lax.rem(y + dy, SIDE) * 2 + c) * width, width)
            grad[:, pl.ds(at, width)] = piece

    tile = slope_ref.shape[1]
    at = pl.multiple_of(i * tile, tile)
    grad_hidden = lax.dot_general(
        grad[...],
        dense[pl.ds(at, tile), :],
        (((1,), (1,)), ((), ())),
        preferred_element_type=F32,
    )
    acts = (
        (grad_hidden * slope_ref[...]).astype(BF16),
        (grad_hidden * silu_ref[...]).astype(BF16),
    )
    for w in range(2):
        term_ref[...] = jnp.dot(normed_t[...], acts[w], preferred_element_type=F32).astype(BF16)

        def place(k, carry, w=w):
            dx = lax.rem(k // SIDE + SIDE - x, SIDE)
            dz = lax.rem(lax.rem(k, SIDE) + SIDE - z, SIDE)
            row = pl.multiple_of(k * BLOCK, BLOCK)
            for half in range(2):
                slot = slot_ref[w * 160 + k * 10 + 2 * i + half]
                color = slot // 2
                first = jnp.where(color == 0, dx, dz)
                second = jnp.where(color == 0, dz, dx)
                to = first * SIDE + second
                s = w * 2 + lax.rem(slot, 2)
                block = term_ref[pl.ds(row, BLOCK), half * BLOCK : (half + 1) * BLOCK]

                @pl.when((slot >= 0) & (color == core))
                def _(to=to, s=s, block=block):
                    keep_ref[to, s] = block

                @pl.when((slot >= 0) & (color != core))
                def _(to=to, s=s, block=block):
                    give_ref[to, s] = block

            return carry

        lax.fori_loop(0, 16, place, 0)


def place_kernel(order_ref, pos_ref, mine, other, down, gate_out, up_out, down_out):
    core = pos_ref[3]
    for w, out in enumerate((gate_out, up_out)):
        out[...] = jnp.zeros_like(out)
        for ref, holder in ((mine, core), (other, 1 - core)):
            for s in range(2):
                j = order_ref[w * SLOTS + 2 * holder + s]

                @pl.when(j >= 0)
                def _(out=out, ref=ref, j=j, s=s, w=w):
                    at = pl.multiple_of(j * BLOCK, BLOCK)
                    out[:, pl.ds(at, BLOCK)] = ref[w * 2 + s].astype(F32)

    down_out[...] = jnp.zeros_like(down_out)
    for s in range(SLOTS):
        j = order_ref[2 * SLOTS + s]

        @pl.when(j >= 0)
        def _(j=j, s=s):
            at = pl.multiple_of(j * BLOCK, BLOCK)
            down_out[pl.ds(at, BLOCK), :] = down[s].astype(F32)


def slots_of(mask):
    blocks = mask.shape[1]
    i = jnp.arange(blocks, dtype=jnp.int32)
    earlier = (i[None, :] < i[:, None]).astype(jnp.int32)
    place = jnp.sum(mask[:, None, :] * earlier[None], axis=2)
    slot = jnp.where(mask == 1, place, -1)
    hit = slot[:, None, :] == jnp.arange(SLOTS, dtype=jnp.int32)[None, :, None]
    order = jnp.sum(jnp.where(hit, i[None, None, :] + 1, 0), axis=2) - 1
    return slot, order


def row_gather(v):
    own, after, low, high, before = ring_gather(v, y_shift)
    across = jnp.concatenate([low, high], axis=0)
    near = core_swap(jnp.stack([own, after, before]))
    far = core_swap(across)
    return own, after, across, before, near, far


def per_device(tokens, teacher, gate_weight, up_weight, down_weight, gate_mask, up_mask, down_mask):
    rows, width = tokens.shape
    hidden_n = gate_weight.shape[1]
    full = width * lax.axis_size("row")
    my_col = lax.axis_index("col")
    my_row = lax.axis_index("row")
    pos = jnp.stack([my_col // SIDE, my_col % SIDE, my_row // 2, my_row % 2]).astype(jnp.int32)
    masks = jnp.concatenate([gate_mask, up_mask, down_mask.T], axis=0)
    slot, order = slots_of(masks)
    my_order = lax.dynamic_index_in_dim(
        order.reshape(3, 16, SLOTS), my_col, 1, keepdims=False
    ).reshape(-1)
    slot = slot.reshape(-1)
    order = order.reshape(-1)
    block4 = jax.ShapeDtypeStruct((4, BLOCK, BLOCK), BF16)

    keep, give, down_packed = pl.pallas_call(
        pack_kernel,
        out_shape=(block4, block4, block4),
        in_specs=[_smem(), _smem(), _vmem(), _vmem(), _vmem()],
        out_specs=(_vmem(),) * 3,
        compiler_params=_params(32),
        name="pack",
    )(my_order, pos, gate_weight, up_weight, down_weight)

    theirs = core_swap(give)
    own1, after1, low1, high1, before1 = ring_gather(jnp.stack([keep, theirs]), _plane_shift(0))
    across1 = jnp.stack([low1[0], high1[0]])
    line = jnp.stack([own1, after1, across1, before1], axis=1)
    own2, after2, low2, high2, before2 = ring_gather(line, _plane_shift(1))
    near2 = core_swap(jnp.stack([own2[1], after2[1], before2[1]]))
    far2 = core_swap(high2[0])
    down_all = lax.all_gather(down_packed, "col", axis=0, tiled=True)

    half_rows = rows // 2
    tok_spec = pl.BlockSpec((half_rows, width), lambda i: (i, 0))
    normed = pl.pallas_call(
        norm_kernel,
        out_shape=jax.ShapeDtypeStruct((rows, full), BF16),
        grid=(2,),
        in_specs=[_smem()]
        + [tok_spec] * 4
        + [pl.BlockSpec((3, half_rows, width), lambda i: (0, i, 0)), tok_spec],
        out_specs=pl.BlockSpec((half_rows, full), lambda i: (i, 0)),
        compiler_params=_params(48),
        name="norm",
    )(pos, *row_gather(tokens))
    normed_t = normed.T

    tile = 256
    steps = hidden_n // tile

    def weight_specs(w):
        five = pl.BlockSpec((1, 4, 2, BLOCK, BLOCK), lambda i: (0, 0, w, 0, 0))
        four = pl.BlockSpec((4, 2, BLOCK, BLOCK), lambda i: (0, w, 0, 0))
        near = pl.BlockSpec((3, 4, 2, BLOCK, BLOCK), lambda i: (0, 0, w, 0, 0))
        return [five, five, four, five, near, four]

    pieces = (own2, after2, low2[0], before2, near2, far2)
    act_spec = pl.BlockSpec((rows, tile), lambda i: (0, i))
    hidden, slope, silu = pl.pallas_call(
        gate_up_kernel,
        out_shape=(
            jax.ShapeDtypeStruct((rows, hidden_n), BF16),
            jax.ShapeDtypeStruct((rows, hidden_n), F32),
            jax.ShapeDtypeStruct((rows, hidden_n), F32),
        ),
        grid=(steps,),
        in_specs=[_smem(), _smem(), pl.BlockSpec((rows, full), lambda i: (0, 0))]
        + weight_specs(0)
        + weight_specs(1),
        out_specs=(act_spec,) * 3,
        scratch_shapes=[pltpu.VMEM((full, hidden_n), BF16)] * 2,
        compiler_params=_params(56),
        name="gate_up",
    )(order, pos, normed, *pieces, *pieces)
    hidden_t = hidden.T

    part_shape = jax.ShapeDtypeStruct((SIDE, rows, width), BF16)
    part_give, part_keep = pl.pallas_call(
        down_kernel,
        out_shape=(part_shape, part_shape),
        grid=(2 * SIDE,),
        in_specs=[
            _smem(),
            _smem(),
            pl.BlockSpec((rows, hidden_n), lambda i: (0, 0)),
            pl.BlockSpec((64, BLOCK, BLOCK), lambda i: (0, 0, 0)),
        ],
        out_specs=(
            pl.BlockSpec((1, rows, width), lambda i: (jnp.minimum(i, SIDE - 1), 0, 0)),
            pl.BlockSpec((1, rows, width), lambda i: (jnp.maximum(i - SIDE, 0), 0, 0)),
        ),
        scratch_shapes=[pltpu.VMEM((hidden_n, full), BF16)],
        compiler_params=_params(48),
        name="down",
    )(order, pos, hidden, down_all)

    got = core_swap(part_give)
    half = rows // 2
    low = y_shift(_add(part_keep[2, :half], got[2, :half]), 1)
    high = y_shift(_add(part_keep[2, half:], got[2, half:]), -1)
    one = part_keep[1].astype(F32) + got[1].astype(F32)
    three = part_keep[3].astype(F32) + got[3].astype(F32)
    to_after = jnp.concatenate([one[:half] + low.astype(F32), one[half:]], axis=0).astype(BF16)
    to_before = jnp.concatenate([three[:half], three[half:] + high.astype(F32)], axis=0).astype(BF16)
    from_before = y_shift(to_after, 1)
    from_after = y_shift(to_before, -1)
    branch = (
        part_keep[0].astype(F32)
        + got[0].astype(F32)
        + from_before.astype(F32)
        + from_after.astype(F32)
    )
    student = (tokens.astype(F32) + branch).astype(BF16)
    grad_scale = 1.0 / math.sqrt(rows * lax.axis_size("col"))
    grad_tile = ((student.astype(F32) - teacher.astype(F32)) * grad_scale).astype(BF16)

    grads = row_gather(grad_tile)
    down_term = pl.pallas_call(
        down_grad_kernel,
        out_shape=jax.ShapeDtypeStruct((64, BLOCK, BLOCK), BF16),
        in_specs=[_smem(), _smem()] + [_vmem()] * 7,
        out_specs=_vmem(),
        compiler_params=_params(48),
        name="down_grad",
    )(slot, pos, hidden_t, *grads)
    down_sum = lax.psum_scatter(down_term, "col", scatter_dimension=0, tiled=True)

    whole = lambda shape: pl.BlockSpec(shape, lambda i: (0,) * len(shape))
    term_shape = jax.ShapeDtypeStruct((16, 4, BLOCK, BLOCK), BF16)
    term_keep, term_give = pl.pallas_call(
        act_grad_kernel,
        out_shape=(term_shape, term_shape),
        grid=(steps,),
        in_specs=[_smem(), _smem(), _smem()]
        + [whole((rows, width))] * 4
        + [whole((3, rows, width)), whole((rows, width)), whole((64, BLOCK, BLOCK))]
        + [act_spec, act_spec, whole((full, rows))],
        out_specs=(whole((16, 4, BLOCK, BLOCK)),) * 2,
        scratch_shapes=[
            pltpu.VMEM((hidden_n, full), BF16),
            pltpu.VMEM((rows, full), BF16),
            pltpu.VMEM((full, tile), BF16),
        ],
        compiler_params=_params(58),
        name="act_grad",
    )(order, slot, pos, *grads, down_all, slope, silu, normed_t)

    term_got = core_swap(term_give)
    mine, theirs = term_keep.reshape(4, 4, 4, BLOCK, BLOCK), term_got.reshape(4, 4, 4, BLOCK, BLOCK)
    for stage in range(2):
        shift = _plane_shift(stage)
        low = shift(mine[2], 1)
        high = shift(theirs[2], -1)
        to_after = jnp.stack([_add(mine[1], low), theirs[1]])
        to_before = jnp.stack([mine[3], _add(theirs[3], high)])
        a = shift(to_after, 1)
        b = shift(to_before, -1)
        mine = mine[0].astype(F32) + a[0].astype(F32) + b[0].astype(F32)
        theirs = theirs[0].astype(F32) + a[1].astype(F32) + b[1].astype(F32)
        if stage == 0:
            mine, theirs = mine.astype(BF16), theirs.astype(BF16)
    other = core_swap(theirs.astype(BF16))

    grad_gate, grad_up, grad_down = pl.pallas_call(
        place_kernel,
        out_shape=(
            jax.ShapeDtypeStruct(gate_weight.shape, F32),
            jax.ShapeDtypeStruct(up_weight.shape, F32),
            jax.ShapeDtypeStruct(down_weight.shape, F32),
        ),
        in_specs=[_smem(), _smem()] + [_vmem()] * 3,
        out_specs=(_vmem(),) * 3,
        compiler_params=_params(32),
        name="place",
    )(my_order, pos, mine, other, down_sum)
    return (student, grad_gate, grad_up, grad_down)


def solution(mesh):
    return jax.shard_map(
        per_device,
        mesh=mesh,
        in_specs=(
            P("col", "row"),
            P("col", "row"),
            P("col", "row"),
            P("col", "row"),
            P("row", "col"),
            P(None, "row"),
            P(None, "row"),
            P("row", None),
        ),
        out_specs=(P("col", "row"), P("col", "row"), P("col", "row"), P("row", "col")),
        check_vma=False,
    )
```

```python
import math

import jax
import jax.numpy as jnp
from jax import lax
from jax.experimental import pallas as pl
from jax.experimental.pallas import tpu as pltpu
from jax.sharding import PartitionSpec as P

BLOCK = 128
EPSILON = 1e-06
SLOTS = 4
SIDE = 4
BF16 = jnp.bfloat16
F32 = jnp.float32


def _row_perm(dy, flip):
    return [
        (y * 2 + c, ((y + dy) % SIDE) * 2 + (c ^ flip)) for y in range(SIDE) for c in range(2)
    ]


def y_shift(v, d):
    return lax.ppermute(v, "row", _row_perm(d, 0))


def core_swap(v):
    return lax.ppermute(v, "row", _row_perm(0, 1))


def _plane_shift(stage):
    def shift(v, d):
        perm = []
        for y in range(SIDE):
            for c in range(2):
                for x in range(SIDE):
                    for z in range(SIDE):
                        if (c == 0) == (stage == 0):
                            tx, tz = (x + d) % SIDE, z
                        else:
                            tx, tz = x, (z + d) % SIDE
                        r = (y * 2 + c) * 16
                        perm.append((r + x * 4 + z, r + tx * 4 + tz))
        return lax.ppermute(v, ("row", "col"), perm)

    return shift


def gather(v, shift):
    return v, shift(v, -1), shift(v, 2), shift(v, 1)


def exchange(parts, shift):
    return [shift(parts[d], d) for d in range(1, SIDE)]


def _params(mib):
    return pltpu.CompilerParams(vmem_limit_bytes=mib << 20)


def _smem():
    return pl.BlockSpec(memory_space=pltpu.SMEM)


def _vmem():
    return pl.BlockSpec(memory_space=pltpu.VMEM)


def _at(index, size):
    return pl.ds(pl.multiple_of(index * size, size), size)


def _place():
    row, col = lax.axis_index("row"), lax.axis_index("col")
    return col >> 2, col & 3, row >> 1, row & 1


def _live(bits):
    order = [jnp.int32(-1)] * SLOTS
    seen = jnp.int32(0)
    for j, bit in enumerate(bits):
        for s in range(SLOTS):
            order[s] = jnp.where((bit == 1) & (seen == s), j, order[s])
        seen = seen + bit
    return order


def pack_kernel(gate_mask, up_mask, down_mask, gate_ref, up_ref, down_ref, pair_out, down_out):
    col = lax.axis_index("col")
    count = gate_ref.shape[1] // BLOCK
    gate_live = _live([gate_mask[col, j] for j in range(count)])
    up_live = _live([up_mask[col, j] for j in range(count)])
    down_live = _live([down_mask[j, col] for j in range(count)])

    def block(ref, j, axis):
        at = _at(jnp.maximum(j, 0), BLOCK)
        v = ref[:, at] if axis else ref[at, :]
        return jnp.where(j >= 0, v, jnp.zeros_like(v))

    for s in range(SLOTS):
        pair_out[s] = block(gate_ref, gate_live[s], 1)
        pair_out[SLOTS + s] = block(up_ref, up_live[s], 1)
        down_out[s] = block(down_ref, down_live[s], 0)


def _row_pieces(refs):
    _, _, y, core = _place()
    for n, ref in enumerate(refs):
        yield ((y + (n & 3)) & 3) * 2 + (core if n < SIDE else 1 - core), ref


def norm_kernel(*refs):
    pieces = list(_row_pieces(refs[:8]))
    out_ref = refs[8]
    width = refs[0].shape[1]
    total = None
    for _, ref in pieces:
        f = ref[...].astype(F32)
        total = f * f if total is None else total + f * f
    mean = jnp.sum(total, axis=1, keepdims=True) * (1.0 / out_ref.shape[1])
    scale = lax.rsqrt(mean + EPSILON)
    for r, ref in pieces:
        out_ref[:, _at(r, width)] = (ref[...].astype(F32) * scale).astype(BF16)


def _tile_at(first, second):
    x, z, _, core = _place()
    dx = jnp.where(core == 0, first, second)
    dz = jnp.where(core == 0, second, first)
    return ((x + dx) & 3) * SIDE + ((z + dz) & 3)


def gate_up_kernel(order_ref, x_ref, *refs):
    pieces = refs[:SIDE]
    hidden_ref, slope_ref, silu_ref, dense = refs[SIDE:]

    @pl.when(pl.program_id(0) == 0)
    def _():
        dense[...] = jnp.zeros_like(dense)
        for second in range(SIDE):
            for first in range(SIDE):
                k = _tile_at(first, second)
                for w in range(2):
                    for s in range(SLOTS):
                        j = order_ref[w * 64 + k * SLOTS + s]
                        block = pieces[second][first, w * SLOTS + s]
                        dense[w, _at(k, BLOCK), _at(j, BLOCK)] = block

    tile = hidden_ref.shape[1]
    cols = _at(pl.program_id(0), tile)
    x = x_ref[...]
    gate = jnp.dot(x, dense[0, :, cols], preferred_element_type=F32)
    up = jnp.dot(x, dense[1, :, cols], preferred_element_type=F32)
    sig = jax.nn.sigmoid(gate)
    silu = gate * sig
    hidden_ref[...] = (silu * up).astype(BF16)
    slope_ref[...] = up * (sig * (1.0 + gate * (1.0 - sig)))
    silu_ref[...] = silu


def _dense_down(order_ref, packed, dense):
    dense[...] = jnp.zeros_like(dense)
    for k in range(16):
        for s in range(SLOTS):
            j = order_ref[128 + k * SLOTS + s]
            dense[_at(j, BLOCK), k * BLOCK : (k + 1) * BLOCK] = packed[k * SLOTS + s]


def down_kernel(order_ref, hidden_ref, packed, give_ref, keep_ref, dense):
    i = pl.program_id(0)

    @pl.when(i == 0)
    def _():
        _dense_down(order_ref, packed, dense)

    _, _, y, core = _place()
    tile = keep_ref.shape[2]

    def part(dy, c):
        cols = _at(((y + dy) & 3) * 2 + c, tile)
        rows = dense[: hidden_ref.shape[1], cols]
        return jnp.dot(hidden_ref[...], rows, preferred_element_type=F32).astype(BF16)

    @pl.when(i < SIDE)
    def _():
        give_ref[0] = part(i, 1 - core)

    @pl.when(i >= SIDE)
    def _():
        keep_ref[0] = part(i - SIDE, core)


def _over_tokens(a, b):
    return lax.dot_general(a, b, (((0,), (0,)), ((), ())), preferred_element_type=F32)


def _pick_blocks(order_ref, weight, block_of, outs, blocks):
    for first in range(SIDE):
        for second in range(SIDE):
            k = _tile_at(first, second)
            for s in range(SLOTS):
                j = jnp.minimum(order_ref[weight * 64 + k * SLOTS + s], blocks - 1)
                outs[first][second, s] = block_of(_at(k, BLOCK), _at(j, BLOCK))


def down_grad_kernel(order_ref, hidden, *refs):
    pieces, outs, terms = refs[:8], refs[8:12], refs[12]
    width = pieces[0].shape[1]
    for r, ref in _row_pieces(pieces):
        terms[:, _at(r, width)] = _over_tokens(hidden[...], ref[...]).astype(BF16)
    blocks = hidden.shape[1] // BLOCK
    _pick_blocks(order_ref, 2, lambda k, j: terms[j, k], outs, blocks)


def gate_grad_kernel(order_ref, *refs):
    pieces = refs[:8]
    packed, slope_ref, silu_ref, normed = refs[8:12]
    outs, act_ref = refs[12:16], refs[16]
    dense, grad, terms = refs[17:]
    i = pl.program_id(0)

    @pl.when(i == 0)
    def _():
        _dense_down(order_ref, packed, dense)
        for r, ref in _row_pieces(pieces):
            grad[:, _at(r, ref.shape[1])] = ref[...]

    tile = act_ref.shape[1]
    grad_hidden = lax.dot_general(
        grad[...], dense[_at(i, tile), :], (((1,), (1,)), ((), ())), preferred_element_type=F32
    )
    act_ref[...] = (grad_hidden * silu_ref[...]).astype(BF16)
    act = (grad_hidden * slope_ref[...]).astype(BF16)
    terms[:, _at(i, tile)] = _over_tokens(normed[...], act).astype(BF16)

    @pl.when(i == pl.num_programs(0) - 1)
    def _():
        blocks = terms.shape[1] // BLOCK
        _pick_blocks(order_ref, 0, lambda k, j: terms[k, j], outs, blocks)


def up_grad_kernel(order_ref, act_ref, normed, *refs):
    outs, terms = refs[:4], refs[4]
    i = pl.program_id(0)
    tile = act_ref.shape[1]
    terms[:, _at(i, tile)] = _over_tokens(normed[...], act_ref[...]).astype(BF16)

    @pl.when(i == pl.num_programs(0) - 1)
    def _():
        blocks = terms.shape[1] // BLOCK
        _pick_blocks(order_ref, 1, lambda k, j: terms[k, j], outs, blocks)


def place_kernel(order_ref, total, gate_out, up_out, down_out):
    col = lax.axis_index("col")
    blocks = gate_out.shape[1] // BLOCK
    for w, out in enumerate((gate_out, up_out, down_out)):
        out[...] = jnp.zeros_like(out)
        for s in range(SLOTS):
            j = order_ref[w * 64 + col * SLOTS + s]

            @pl.when(j < blocks)
            def _(out=out, j=j, w=w, s=s):
                if w == 2:
                    out[_at(j, BLOCK), :] = total[w * SLOTS + s]
                else:
                    out[:, _at(j, BLOCK)] = total[w * SLOTS + s]


def live_order(mask):
    blocks = mask.shape[1]
    i = jnp.arange(blocks, dtype=jnp.int32)
    earlier = (i[None, :] < i[:, None]).astype(jnp.int32)
    place = jnp.sum(mask[:, None, :] * earlier[None], axis=2)
    slot = jnp.where(mask == 1, place, -1)
    hit = slot[:, None, :] == jnp.arange(SLOTS, dtype=jnp.int32)[None, :, None]
    return blocks + jnp.sum(jnp.where(hit, i[None, None, :] - blocks, 0), axis=2)


def row_spread(four):
    return (*four, *(core_swap(v) for v in four))


def per_device(tokens, teacher, gate_weight, up_weight, down_weight, gate_mask, up_mask, down_mask):
    rows, width = tokens.shape
    hidden_n = gate_weight.shape[1]
    full = width * lax.axis_size("row")
    half = rows // 2
    order = live_order(jnp.concatenate([gate_mask, up_mask, down_mask.T], axis=0)).reshape(-1)
    block_shape = lambda *lead: jax.ShapeDtypeStruct((*lead, BLOCK, BLOCK), BF16)

    tok = gather(tokens, y_shift)
    pair, down_packed = pl.pallas_call(
        pack_kernel,
        out_shape=(block_shape(2 * SLOTS), block_shape(SLOTS)),
        in_specs=[_smem()] * 3 + [_vmem()] * 3,
        out_specs=(_vmem(),) * 2,
        compiler_params=_params(32),
        name="pack",
    )(gate_mask, up_mask, down_mask, gate_weight, up_weight, down_weight)

    line = jnp.stack(gather(pair, _plane_shift(0)))
    weights = gather(line, _plane_shift(1))
    down_all = lax.all_gather(down_packed, "col", axis=0, tiled=True)

    tok_spec = pl.BlockSpec((half, width), lambda i: (i, 0))
    normed = pl.pallas_call(
        norm_kernel,
        out_shape=jax.ShapeDtypeStruct((rows, full), BF16),
        grid=(2,),
        in_specs=[tok_spec] * 8,
        out_specs=pl.BlockSpec((half, full), lambda i: (i, 0)),
        compiler_params=_params(48),
        name="norm",
    )(*row_spread(tok))

    tile = 256
    steps = hidden_n // tile
    whole = lambda *shape: pl.BlockSpec(shape, lambda i: (0,) * len(shape))
    act_spec = pl.BlockSpec((rows, tile), lambda i: (0, i))
    hidden, slope, silu = pl.pallas_call(
        gate_up_kernel,
        out_shape=(
            jax.ShapeDtypeStruct((rows, hidden_n), BF16),
            jax.ShapeDtypeStruct((rows, hidden_n), F32),
            jax.ShapeDtypeStruct((rows, hidden_n), F32),
        ),
        grid=(steps,),
        in_specs=[_smem(), whole(rows, full)] + [whole(SIDE, 2 * SLOTS, BLOCK, BLOCK)] * SIDE,
        out_specs=(act_spec,) * 3,
        scratch_shapes=[pltpu.VMEM((2, full, hidden_n + BLOCK), BF16)],
        compiler_params=_params(56),
        name="gate_up",
    )(order, normed, *weights)

    dense_down = pltpu.VMEM((hidden_n + BLOCK, full), BF16)
    part_shape = jax.ShapeDtypeStruct((SIDE, rows, width), BF16)
    part_give, part_keep = pl.pallas_call(
        down_kernel,
        out_shape=(part_shape, part_shape),
        grid=(2 * SIDE,),
        in_specs=[_smem(), whole(rows, hidden_n), whole(16 * SLOTS, BLOCK, BLOCK)],
        out_specs=(
            pl.BlockSpec((1, rows, width), lambda i: (jnp.minimum(i, SIDE - 1), 0, 0)),
            pl.BlockSpec((1, rows, width), lambda i: (jnp.maximum(i - SIDE, 0), 0, 0)),
        ),
        scratch_shapes=[dense_down],
        compiler_params=_params(48),
        name="down",
    )(order, hidden, down_all)

    got = core_swap(part_give)
    parts = [part_keep[d].astype(F32) + got[d].astype(F32) for d in range(SIDE)]
    branch = parts[0]
    for v in exchange([p.astype(BF16) for p in parts], y_shift):
        branch = branch + v.astype(F32)
    student = (tokens.astype(F32) + branch).astype(BF16)
    grad_scale = 1.0 / math.sqrt(rows * lax.axis_size("col"))
    grad_tile = ((student.astype(F32) - teacher.astype(F32)) * grad_scale).astype(BF16)
    grads = row_spread(gather(grad_tile, y_shift))

    first, second = _plane_shift(0), _plane_shift(1)
    term_shapes = (block_shape(SIDE, SLOTS),) * SIDE
    down_terms = pl.pallas_call(
        down_grad_kernel,
        out_shape=term_shapes,
        in_specs=[_smem()] + [_vmem()] * 9,
        out_specs=(_vmem(),) * SIDE,
        scratch_shapes=[pltpu.VMEM((hidden_n, full), BF16)],
        compiler_params=_params(48),
        name="down_grad",
    )(order, hidden, *grads)
    *down_terms, normed = lax.optimization_barrier((*down_terms, normed))
    down_got = exchange(down_terms, first)

    term_spec = whole(SIDE, SLOTS, BLOCK, BLOCK)
    piece = whole(rows, width)
    *gate_terms, act_up = pl.pallas_call(
        gate_grad_kernel,
        out_shape=(*term_shapes, jax.ShapeDtypeStruct((rows, hidden_n), BF16)),
        grid=(steps,),
        in_specs=[_smem()]
        + [piece] * 8
        + [whole(16 * SLOTS, BLOCK, BLOCK), act_spec, act_spec, whole(rows, full)],
        out_specs=(*(term_spec,) * SIDE, act_spec),
        scratch_shapes=[
            dense_down,
            pltpu.VMEM((rows, full), BF16),
            pltpu.VMEM((full, hidden_n), BF16),
        ],
        compiler_params=_params(56),
        name="gate_grad",
    )(order, *grads, down_all, slope, silu, normed)
    gate_got = exchange(gate_terms, first)
    act_up, *down_got = lax.optimization_barrier((act_up, *down_got))
    up_terms = pl.pallas_call(
        up_grad_kernel,
        out_shape=term_shapes,
        grid=(steps,),
        in_specs=[_smem(), act_spec, whole(rows, full)],
        out_specs=(term_spec,) * SIDE,
        scratch_shapes=[pltpu.VMEM((full, hidden_n), BF16)],
        compiler_params=_params(48),
        name="up_grad",
    )(order, act_up, normed)
    up_got = exchange(up_terms, first)

    sums = [
        sum((v.astype(F32) for v in got), own[0].astype(F32))
        for own, got in ((gate_terms, gate_got), (up_terms, up_got), (down_terms, down_got))
    ]
    parts = [jnp.concatenate([v[d] for v in sums]) for d in range(SIDE)]
    total = parts[0]
    for v in exchange([p.astype(BF16) for p in parts], second):
        total = total + v.astype(F32)

    grad_gate, grad_up, grad_down = pl.pallas_call(
        place_kernel,
        out_shape=(
            jax.ShapeDtypeStruct(gate_weight.shape, F32),
            jax.ShapeDtypeStruct(up_weight.shape, F32),
            jax.ShapeDtypeStruct(down_weight.shape, F32),
        ),
        in_specs=[_smem(), _vmem()],
        out_specs=(_vmem(),) * 3,
        compiler_params=_params(32),
        name="place",
    )(order, total)
    return (student, grad_gate, grad_up, grad_down)


def solution(mesh):
    return jax.shard_map(
        per_device,
        mesh=mesh,
        in_specs=(
            P("col", "row"),
            P("col", "row"),
            P("col", "row"),
            P("col", "row"),
            P("row", "col"),
            P(None, "row"),
            P(None, "row"),
            P("row", None),
        ),
        out_specs=(P("col", "row"), P("col", "row"), P("col", "row"), P("row", "col")),
        check_vma=False,
    )
```

```python
import math

import jax
import jax.numpy as jnp
from jax import lax
from jax.experimental import pallas as pl
from jax.experimental.pallas import tpu as pltpu
from jax.sharding import PartitionSpec as P

BLOCK = 128
EPSILON = 1e-06
SLOTS = 4
SIDE = 4
TILE = 256
BF16 = jnp.bfloat16
F32 = jnp.float32


def _row_perm(dy, flip):
    return [
        (y * 2 + c, ((y + dy) % SIDE) * 2 + (c ^ flip)) for y in range(SIDE) for c in range(2)
    ]


def y_shift(v, d):
    return lax.ppermute(v, "row", _row_perm(d, 0))


def core_swap(v):
    return lax.ppermute(v, "row", _row_perm(0, 1))


def _plane_shift(stage):
    def shift(v, d):
        perm = []
        for y in range(SIDE):
            for c in range(2):
                for x in range(SIDE):
                    for z in range(SIDE):
                        if (c == 0) == (stage == 0):
                            tx, tz = (x + d) % SIDE, z
                        else:
                            tx, tz = x, (z + d) % SIDE
                        r = (y * 2 + c) * 16
                        perm.append((r + x * 4 + z, r + tx * 4 + tz))
        return lax.ppermute(v, ("row", "col"), perm)

    return shift


def gather(v, shift):
    return v, shift(v, -1), shift(v, 2), shift(v, 1)


def exchange(parts, shift):
    return [shift(parts[d], d) for d in range(1, SIDE)]


def _call(kernel, shapes, name, mib, scratch=(), tables=0, far=(), far_out=()):
    def run(*operands):
        smem = pl.BlockSpec(memory_space=pltpu.SMEM)
        vmem = pl.BlockSpec(memory_space=pltpu.VMEM)
        anywhere = pl.BlockSpec(memory_space=pltpu.HBM)
        specs = [smem if n < tables else vmem for n in range(len(operands))]
        return pl.pallas_call(
            kernel,
            out_shape=tuple(
                pltpu.HBM(v.shape, v.dtype) if n in far_out else v for n, v in enumerate(shapes)
            ),
            in_specs=[anywhere if n in far else spec for n, spec in enumerate(specs)],
            out_specs=tuple(anywhere if n in far_out else vmem for n in range(len(shapes))),
            scratch_shapes=list(scratch),
            compiler_params=pltpu.CompilerParams(vmem_limit_bytes=mib << 20),
            name=name,
        )(
            *(
                pltpu.with_memory_space_constraint(v, pltpu.HBM) if n in far else v
                for n, v in enumerate(operands)
            )
        )

    return run


def _at(index, size):
    return pl.ds(pl.multiple_of(index * size, size), size)


def _place():
    row, col = lax.axis_index("row"), lax.axis_index("col")
    return col >> 2, col & 3, row >> 1, row & 1


def _live(bits):
    order = [jnp.int32(-1)] * SLOTS
    seen = jnp.int32(0)
    for j, bit in enumerate(bits):
        for s in range(SLOTS):
            order[s] = jnp.where((bit == 1) & (seen == s), j, order[s])
        seen = seen + bit
    return order


def pack_kernel(*refs):
    sources, out_ref, copies, sems = refs[:6], refs[6], refs[7:13], refs[13]
    loads = [
        pltpu.make_async_copy(src, dst, sems.at[n])
        for n, (src, dst) in enumerate(zip(sources, copies))
    ]
    for load in loads:
        load.start()
    for load in loads:
        load.wait()
    gate_mask, up_mask, down_mask, gate_ref, up_ref, down_ref = copies
    col = lax.axis_index("col")
    count = gate_ref.shape[1] // BLOCK
    gate_live = _live([gate_mask[col, j] for j in range(count)])
    up_live = _live([up_mask[col, j] for j in range(count)])
    down_live = _live([down_mask[j, col] for j in range(count)])

    def block(ref, j, axis):
        at = _at(jnp.maximum(j, 0), BLOCK)
        v = ref[:, at] if axis else ref[at, :]
        return jnp.where(j >= 0, v, jnp.zeros_like(v))

    for s in range(SLOTS):
        out_ref[s] = block(gate_ref, gate_live[s], 1)
        out_ref[SLOTS + s] = block(up_ref, up_live[s], 1)
        out_ref[2 * SLOTS + s] = block(down_ref, down_live[s], 0)


def _row_pieces(refs):
    _, _, y, core = _place()
    for n, ref in enumerate(refs):
        yield ((y + (n & 3)) & 3) * 2 + (core if n < SIDE else 1 - core), ref


def norm_kernel(*refs):
    pieces = list(_row_pieces(refs[:8]))
    out_ref, turned_ref = refs[8:]
    width = refs[0].shape[1]
    total = None
    for _, ref in pieces:
        f = ref[...].astype(F32)
        total = f * f if total is None else total + f * f
    mean = jnp.sum(total, axis=1, keepdims=True) * (1.0 / out_ref.shape[1])
    scale = lax.rsqrt(mean + EPSILON)
    for r, ref in pieces:
        normed = (ref[...].astype(F32) * scale).astype(BF16)
        out_ref[:, _at(r, width)] = normed
        turned_ref[_at(r, width), :] = normed.T


def _tile_at(first, second):
    x, z, _, core = _place()
    dx = jnp.where(core == 0, first, second)
    dz = jnp.where(core == 0, second, first)
    return ((x + dx) & 3) * SIDE + ((z + dz) & 3)


def gate_up_kernel(order_ref, x_ref, *refs):
    pieces = refs[:SIDE]
    hidden_ref, slope_out, silu_out, dense, packed, slope, silu, in_sems, out_sems = refs[SIDE:]
    loads = [
        pltpu.make_async_copy(pieces[n], packed.at[n], in_sems.at[n]) for n in range(SIDE)
    ]
    for load in loads:
        load.start()
    dense[...] = jnp.zeros_like(dense)
    for second in range(SIDE):
        loads[second].wait()
        for first in range(SIDE):
            k = _tile_at(first, second)
            for w in range(2):
                for s in range(SLOTS):
                    j = order_ref[w * 64 + k * SLOTS + s]
                    block = packed[second, first, w * SLOTS + s]
                    dense[w, _at(k, BLOCK), _at(j, BLOCK)] = block
    stores = []
    for n in range(0, hidden_ref.shape[1], TILE):
        cols = slice(n, n + TILE)
        gate = jnp.dot(x_ref[...], dense[0, :, cols], preferred_element_type=F32)
        up = jnp.dot(x_ref[...], dense[1, :, cols], preferred_element_type=F32)
        sig = jax.nn.sigmoid(gate)
        act = gate * sig
        hidden_ref[:, cols] = (act * up).astype(BF16)
        slope[:, cols] = (up * (sig * (1.0 + gate * (1.0 - sig)))).astype(BF16)
        silu[:, cols] = act.astype(BF16)
        for w, (src, dst) in enumerate(((slope, slope_out), (silu, silu_out))):
            stores.append(
                pltpu.make_async_copy(
                    src.at[:, cols], dst.at[:, cols], out_sems.at[w, n // TILE]
                )
            )
            stores[-1].start()
    for store in stores:
        store.wait()


def _down_part(hidden_ref, dense, out_ref, core):
    y = _place()[2]
    width = out_ref.shape[2]
    for dy in range(SIDE):
        rows = dense[: hidden_ref.shape[1], _at(((y + dy) & 3) * 2 + core, width)]
        out_ref[dy] = jnp.dot(hidden_ref[...], rows, preferred_element_type=F32).astype(BF16)


def down_give_kernel(order_ref, hidden_ref, *refs):
    pieces, (give_ref, dense, packed, sems) = refs[:SIDE], refs[SIDE:]
    loads = [pltpu.make_async_copy(pieces[n], packed.at[n], sems.at[n]) for n in range(SIDE)]
    for load in loads:
        load.start()
    dense[...] = jnp.zeros_like(dense)
    for second in range(SIDE):
        loads[second].wait()
        for first in range(SIDE):
            k = _tile_at(first, second)
            for s in range(SLOTS):
                j = order_ref[128 + k * SLOTS + s]
                dense[_at(j, BLOCK), _at(k, BLOCK)] = packed[second, first, s]
    _down_part(hidden_ref, dense, give_ref, 1 - _place()[3])


def down_keep_kernel(hidden_ref, dense, keep_ref):
    _down_part(hidden_ref, dense, keep_ref, _place()[3])


def turn_kernel(x_ref, out_ref):
    out_ref[...] = x_ref[...].T


def _pick_blocks(order_ref, weight, block_of, outs, blocks):
    for first in range(SIDE):
        for second in range(SIDE):
            k = _tile_at(first, second)
            for s in range(SLOTS):
                j = jnp.minimum(order_ref[weight * 64 + k * SLOTS + s], blocks - 1)
                outs[first][second, s] = block_of(_at(k, BLOCK), _at(j, BLOCK))


def down_grad_kernel(order_ref, hidden_t, *refs):
    pieces, outs, terms = refs[:8], refs[8:12], refs[12]
    width = pieces[0].shape[1]
    for r, ref in _row_pieces(pieces):
        term = jnp.dot(hidden_t[...], ref[...], preferred_element_type=F32)
        terms[:, _at(r, width)] = term.astype(BF16)
    blocks = hidden_t.shape[0] // BLOCK
    _pick_blocks(order_ref, 2, lambda k, j: terms[j, k], outs, blocks)


def _term_blocks(order_ref, weight, normed_t, act_ref, outs, terms):
    terms[...] = jnp.dot(normed_t[...], act_ref[...], preferred_element_type=F32).astype(BF16)
    blocks = terms.shape[1] // BLOCK
    _pick_blocks(order_ref, weight, lambda k, j: terms[k, j], outs, blocks)


def gate_grad_kernel(order_ref, *refs):
    pieces = refs[:8]
    dense, slope_ref, silu_ref, normed_t = refs[8:12]
    outs, up_act = refs[12:16], refs[16]
    grad, gate_act, terms = refs[17:]
    for r, ref in _row_pieces(pieces):
        grad[:, _at(r, ref.shape[1])] = ref[...]
    for n in range(0, up_act.shape[1], TILE):
        cols = slice(n, n + TILE)
        grad_hidden = lax.dot_general(
            grad[...], dense[cols, :], (((1,), (1,)), ((), ())), preferred_element_type=F32
        )
        up_act[:, cols] = (grad_hidden * silu_ref[:, cols]).astype(BF16)
        gate_act[:, cols] = (grad_hidden * slope_ref[:, cols]).astype(BF16)
    _term_blocks(order_ref, 0, normed_t, gate_act, outs, terms)


def up_grad_kernel(order_ref, act_ref, normed_t, *refs):
    _term_blocks(order_ref, 1, normed_t, act_ref, refs[:4], refs[4])


def place_kernel(order_ref, total, gate_out, up_out, down_out):
    col = lax.axis_index("col")
    blocks = gate_out.shape[1] // BLOCK
    for w, out in enumerate((gate_out, up_out, down_out)):
        out[...] = jnp.zeros_like(out)
        for s in range(SLOTS):
            j = order_ref[w * 64 + col * SLOTS + s]

            @pl.when(j < blocks)
            def _(out=out, j=j, w=w, s=s):
                if w == 2:
                    out[_at(j, BLOCK), :] = total[w * SLOTS + s]
                else:
                    out[:, _at(j, BLOCK)] = total[w * SLOTS + s]


def live_order(mask):
    blocks = mask.shape[1]
    i = jnp.arange(blocks, dtype=jnp.int32)
    earlier = (i[None, :] < i[:, None]).astype(jnp.int32)
    place = jnp.sum(mask[:, None, :] * earlier[None], axis=2)
    slot = jnp.where(mask == 1, place, -1)
    hit = slot[:, None, :] == jnp.arange(SLOTS, dtype=jnp.int32)[None, :, None]
    return blocks + jnp.sum(jnp.where(hit, i[None, None, :] - blocks, 0), axis=2)


def row_spread(four):
    return (*four, *(core_swap(v) for v in four))


def per_device(tokens, teacher, gate_weight, up_weight, down_weight, gate_mask, up_mask, down_mask):
    rows, width = tokens.shape
    hidden_n = gate_weight.shape[1]
    full = width * lax.axis_size("row")
    order = live_order(jnp.concatenate([gate_mask, up_mask, down_mask.T], axis=0)).reshape(-1)
    block_shape = lambda *lead: jax.ShapeDtypeStruct((*lead, BLOCK, BLOCK), BF16)

    tok = gather(tokens, y_shift)
    (live,) = _call(
        pack_kernel, (block_shape(3 * SLOTS),), "pack", 8,
        [pltpu.SMEM(m.shape, m.dtype) for m in (gate_mask, up_mask, down_mask)]
        + [pltpu.VMEM(w.shape, w.dtype) for w in (gate_weight, up_weight, down_weight)]
        + [pltpu.SemaphoreType.DMA((6,))],
        far=range(6),
    )(gate_mask, up_mask, down_mask, gate_weight, up_weight, down_weight)

    lines = gather(live, _plane_shift(0))
    weights = gather(jnp.stack([v[: 2 * SLOTS] for v in lines]), _plane_shift(1))
    line = jnp.stack([v[2 * SLOTS :] for v in lines])
    downs = gather(line, _plane_shift(1))

    normed, normed_t = _call(
        norm_kernel,
        (jax.ShapeDtypeStruct((rows, full), BF16), jax.ShapeDtypeStruct((full, rows), BF16)),
        "norm",
        20,
    )(*row_spread(tok))

    act_shape = jax.ShapeDtypeStruct((rows, hidden_n), BF16)
    hidden, slope, silu = _call(
        gate_up_kernel,
        (act_shape,) * 3,
        "gate_up",
        34,
        [
            pltpu.VMEM((2, full, hidden_n + BLOCK), BF16),
            pltpu.VMEM((SIDE, SIDE, 2 * SLOTS, BLOCK, BLOCK), BF16),
            pltpu.VMEM((rows, hidden_n), BF16),
            pltpu.VMEM((rows, hidden_n), BF16),
            pltpu.SemaphoreType.DMA((SIDE,)),
            pltpu.SemaphoreType.DMA((2, hidden_n // TILE)),
        ],
        1,
        far=range(2, 2 + SIDE),
        far_out=(1, 2),
    )(order, normed, *weights)

    part_shape = jax.ShapeDtypeStruct((SIDE, rows, width), BF16)
    part_give, dense_down = _call(
        down_give_kernel,
        (part_shape, jax.ShapeDtypeStruct((hidden_n + BLOCK, full), BF16)),
        "down_give",
        16,
        [
            pltpu.VMEM((SIDE, SIDE, SLOTS, BLOCK, BLOCK), BF16),
            pltpu.SemaphoreType.DMA((SIDE,)),
        ],
        1,
        far=range(2, 2 + SIDE),
    )(order, hidden, *downs)
    (part_keep,) = _call(down_keep_kernel, (part_shape,), "down_keep", 16)(hidden, dense_down)
    (hidden_t,) = _call(
        turn_kernel, (jax.ShapeDtypeStruct((hidden_n, rows), BF16),), "turn", 16
    )(hidden)

    got = core_swap(part_give)
    parts = [part_keep[d].astype(F32) + got[d].astype(F32) for d in range(SIDE)]
    branch = parts[0]
    for v in exchange([p.astype(BF16) for p in parts], y_shift):
        branch = branch + v.astype(F32)
    student = (tokens.astype(F32) + branch).astype(BF16)
    grad_scale = 1.0 / math.sqrt(rows * lax.axis_size("col"))
    grad_tile = ((student.astype(F32) - teacher.astype(F32)) * grad_scale).astype(BF16)
    grads = row_spread(gather(grad_tile, y_shift))

    first, second = _plane_shift(0), _plane_shift(1)
    term_shapes = (block_shape(SIDE, SLOTS),) * SIDE
    down_terms = _call(
        down_grad_kernel,
        term_shapes,
        "down_grad",
        16,
        [pltpu.VMEM((hidden_n, full), BF16)],
        1,
    )(order, hidden_t, *grads)
    *down_terms, normed_t = lax.optimization_barrier((*down_terms, normed_t))
    down_got = exchange(down_terms, first)

    *gate_terms, up_act = _call(
        gate_grad_kernel,
        (*term_shapes, act_shape),
        "gate_grad",
        28,
        [
            pltpu.VMEM((rows, full), BF16),
            pltpu.VMEM((rows, hidden_n), BF16),
            pltpu.VMEM((full, hidden_n), BF16),
        ],
        1,
    )(order, *grads, dense_down, slope, silu, normed_t)
    gate_got = exchange(gate_terms, first)
    up_act, *down_got = lax.optimization_barrier((up_act, *down_got))
    up_terms = _call(
        up_grad_kernel, term_shapes, "up_grad", 24, [pltpu.VMEM((full, hidden_n), BF16)], 1
    )(order, up_act, normed_t)
    up_got = exchange(up_terms, first)

    sums = [
        sum((v.astype(F32) for v in got), own[0].astype(F32))
        for own, got in ((gate_terms, gate_got), (up_terms, up_got), (down_terms, down_got))
    ]
    parts = [jnp.concatenate([v[d] for v in sums]) for d in range(SIDE)]
    total = parts[0]
    for v in exchange([p.astype(BF16) for p in parts], second):
        total = total + v.astype(F32)

    grads_out = [
        jax.ShapeDtypeStruct(w.shape, F32) for w in (gate_weight, up_weight, down_weight)
    ]
    grad_gate, grad_up, grad_down = _call(place_kernel, grads_out, "place", 8, [], 1)(order, total)
    return (student, grad_gate, grad_up, grad_down)


def solution(mesh):
    return jax.shard_map(
        per_device,
        mesh=mesh,
        in_specs=(
            P("col", "row"),
            P("col", "row"),
            P("col", "row"),
            P("col", "row"),
            P("row", "col"),
            P(None, "row"),
            P(None, "row"),
            P("row", None),
        ),
        out_specs=(P("col", "row"), P("col", "row"), P("col", "row"), P("row", "col")),
        check_vma=False,
    )
```

```python
import math

import jax
import jax.numpy as jnp
from jax import lax
from jax.experimental import pallas as pl
from jax.experimental.pallas import tpu as pltpu
from jax.sharding import PartitionSpec as P

BLOCK = 128
EPSILON = 1e-06
SLOTS = 4
SIDE = 4
TILE = 256
BF16 = jnp.bfloat16
F32 = jnp.float32


def _row_perm(dy, flip):
    return [
        (y * 2 + c, ((y + dy) % SIDE) * 2 + (c ^ flip)) for y in range(SIDE) for c in range(2)
    ]


def y_shift(v, d):
    return lax.ppermute(v, "row", _row_perm(d, 0))


def y_pass(v):
    perm = [
        (y * 2 + c, ((y + 1 - 2 * c) % SIDE) * 2 + c) for y in range(SIDE) for c in range(2)
    ]
    return lax.ppermute(v, "row", perm)


def core_swap(v):
    return lax.ppermute(v, "row", _row_perm(0, 1))


def _plane_shift(stage):
    def shift(v, d):
        perm = []
        for y in range(SIDE):
            for c in range(2):
                for x in range(SIDE):
                    for z in range(SIDE):
                        if (c == 0) == (stage == 0):
                            tx, tz = (x + d) % SIDE, z
                        else:
                            tx, tz = x, (z + d) % SIDE
                        r = (y * 2 + c) * 16
                        perm.append((r + x * 4 + z, r + tx * 4 + tz))
        return lax.ppermute(v, ("row", "col"), perm)

    return shift


def gather(v, shift):
    return v, shift(v, -1), shift(v, 2), shift(v, 1)


def exchange(parts, shift):
    return [shift(parts[d], d) for d in range(1, SIDE)]


def _call(kernel, shapes, name, mib, scratch=(), tables=0, far=(), far_out=()):
    def run(*operands):
        smem = pl.BlockSpec(memory_space=pltpu.SMEM)
        vmem = pl.BlockSpec(memory_space=pltpu.VMEM)
        anywhere = pl.BlockSpec(memory_space=pltpu.HBM)
        specs = [smem if n < tables else vmem for n in range(len(operands))]
        return pl.pallas_call(
            kernel,
            out_shape=tuple(
                pltpu.HBM(v.shape, v.dtype) if n in far_out else v for n, v in enumerate(shapes)
            ),
            in_specs=[anywhere if n in far else spec for n, spec in enumerate(specs)],
            out_specs=tuple(anywhere if n in far_out else vmem for n in range(len(shapes))),
            scratch_shapes=list(scratch),
            compiler_params=pltpu.CompilerParams(vmem_limit_bytes=mib << 20),
            name=name,
        )(
            *(
                pltpu.with_memory_space_constraint(v, pltpu.HBM) if n in far else v
                for n, v in enumerate(operands)
            )
        )

    return run


def _at(index, size):
    return pl.ds(pl.multiple_of(index * size, size), size)


def _place():
    row, col = lax.axis_index("row"), lax.axis_index("col")
    return col >> 2, col & 3, row >> 1, row & 1


def _live(bits):
    order = [jnp.int32(-1)] * SLOTS
    seen = jnp.int32(0)
    for j, bit in enumerate(bits):
        for s in range(SLOTS):
            order[s] = jnp.where((bit == 1) & (seen == s), j, order[s])
        seen = seen + bit
    return order


def pack_kernel(*refs):
    sources, out_ref, copies, sems = refs[:6], refs[6], refs[7:13], refs[13]
    loads = [
        pltpu.make_async_copy(src, dst, sems.at[n])
        for n, (src, dst) in enumerate(zip(sources, copies))
    ]
    for load in loads:
        load.start()
    for load in loads:
        load.wait()
    gate_mask, up_mask, down_mask, gate_ref, up_ref, down_ref = copies
    col = lax.axis_index("col")
    count = gate_ref.shape[1] // BLOCK
    gate_live = _live([gate_mask[col, j] for j in range(count)])
    up_live = _live([up_mask[col, j] for j in range(count)])
    down_live = _live([down_mask[j, col] for j in range(count)])

    def block(ref, j, axis):
        at = _at(jnp.maximum(j, 0), BLOCK)
        v = ref[:, at] if axis else ref[at, :]
        return jnp.where(j >= 0, v, jnp.zeros_like(v))

    for s in range(SLOTS):
        out_ref[s] = block(gate_ref, gate_live[s], 1)
        out_ref[SLOTS + s] = block(up_ref, up_live[s], 1)
        out_ref[2 * SLOTS + s] = block(down_ref, down_live[s], 0)


def _row_pieces(refs):
    _, _, y, core = _place()
    for n, ref in enumerate(refs):
        yield ((y + (n & 3)) & 3) * 2 + (core if n < SIDE else 1 - core), ref


def norm_kernel(pair, near, near_swapped, far, far_swapped, out_ref, turned_ref):
    _, _, y, core = _place()
    width, half = pair.shape[2], far.shape[1]
    step = 1 - 2 * core
    for n in range(2):
        mine, theirs = core ^ n, core ^ n ^ 1
        at = lambda dy, c: _at(((y + SIDE + dy) & 3) * 2 + c, width)
        out_ref[:, at(0, mine)] = pair[n]
        out_ref[:, at(-step, mine)] = near[n]
        out_ref[:, at(step, theirs)] = near_swapped[n]
        out_ref[_at(core, half), at(2, mine)] = far[n]
        out_ref[_at(1 - core, half), at(2, theirs)] = far_swapped[n]
    total = None
    for n in range(0, out_ref.shape[1], TILE):
        f = out_ref[:, n : n + TILE].astype(F32)
        total = f * f if total is None else total + f * f
    mean = jnp.sum(total, axis=1, keepdims=True) * (1.0 / out_ref.shape[1])
    scale = lax.rsqrt(mean + EPSILON)
    for n in range(0, out_ref.shape[1], TILE):
        normed = (out_ref[:, n : n + TILE].astype(F32) * scale).astype(BF16)
        out_ref[:, n : n + TILE] = normed
        turned_ref[n : n + TILE, :] = normed.T


def _tile_at(first, second):
    x, z, _, core = _place()
    dx = jnp.where(core == 0, first, second)
    dz = jnp.where(core == 0, second, first)
    return ((x + dx) & 3) * SIDE + ((z + dz) & 3)


def gate_up_kernel(order_ref, x_in, *refs):
    pieces = refs[:SIDE]
    hidden_ref, slope_out, silu_out, *scratch = refs[SIDE:]
    dense, packed, x_ref, slope, silu, in_sems, out_sems = scratch
    loads = [
        pltpu.make_async_copy(pieces[n], packed.at[n], in_sems.at[n]) for n in range(SIDE)
    ]
    loads.append(pltpu.make_async_copy(x_in, x_ref, in_sems.at[SIDE]))
    for load in loads:
        load.start()
    dense[...] = jnp.zeros_like(dense)
    for second in range(SIDE):
        loads[second].wait()
        for first in range(SIDE):
            k = _tile_at(first, second)
            for w in range(2):
                for s in range(SLOTS):
                    j = order_ref[w * 64 + k * SLOTS + s]
                    block = packed[second, first, w * SLOTS + s]
                    dense[w, _at(k, BLOCK), _at(j, BLOCK)] = block
    loads[SIDE].wait()
    stores = []
    for n in range(0, hidden_ref.shape[1], TILE):
        cols = slice(n, n + TILE)
        gate = jnp.dot(x_ref[...], dense[0, :, cols], preferred_element_type=F32)
        up = jnp.dot(x_ref[...], dense[1, :, cols], preferred_element_type=F32)
        sig = jax.nn.sigmoid(gate)
        act = gate * sig
        hidden_ref[:, cols] = (act * up).astype(BF16)
        slope[:, cols] = (up * (sig * (1.0 + gate * (1.0 - sig)))).astype(BF16)
        silu[:, cols] = act.astype(BF16)
        for w, (src, dst) in enumerate(((slope, slope_out), (silu, silu_out))):
            stores.append(
                pltpu.make_async_copy(
                    src.at[:, cols], dst.at[:, cols], out_sems.at[w, n // TILE]
                )
            )
            stores[-1].start()
    for store in stores:
        store.wait()


def _down_part(hidden_ref, dense, out_ref, core):
    y = _place()[2]
    width = out_ref.shape[2]
    for dy in range(SIDE):
        rows = dense[: hidden_ref.shape[1], _at(((y + dy) & 3) * 2 + core, width)]
        out_ref[dy] = jnp.dot(hidden_ref[...], rows, preferred_element_type=F32).astype(BF16)


def down_give_kernel(order_ref, hidden_ref, *refs):
    pieces, (give_ref, dense, packed, sems) = refs[:SIDE], refs[SIDE:]
    loads = [pltpu.make_async_copy(pieces[n], packed.at[n], sems.at[n]) for n in range(SIDE)]
    for load in loads:
        load.start()
    dense[...] = jnp.zeros_like(dense)
    for second in range(SIDE):
        loads[second].wait()
        for first in range(SIDE):
            k = _tile_at(first, second)
            for s in range(SLOTS):
                j = order_ref[128 + k * SLOTS + s]
                dense[_at(j, BLOCK), _at(k, BLOCK)] = packed[second, first, s]
    _down_part(hidden_ref, dense, give_ref, 1 - _place()[3])


def down_keep_kernel(hidden_ref, dense, keep_ref):
    _down_part(hidden_ref, dense, keep_ref, _place()[3])


def turn_kernel(x_ref, out_ref):
    out_ref[...] = x_ref[...].T


def _pick_blocks(order_ref, weight, block_of, outs, blocks):
    for first in range(SIDE):
        for second in range(SIDE):
            k = _tile_at(first, second)
            for s in range(SLOTS):
                j = jnp.minimum(order_ref[weight * 64 + k * SLOTS + s], blocks - 1)
                outs[first][second, s] = block_of(_at(k, BLOCK), _at(j, BLOCK))


def down_grad_kernel(order_ref, hidden_t, *refs):
    pieces, outs, terms = refs[:8], refs[8:12], refs[12]
    width = pieces[0].shape[1]
    for r, ref in _row_pieces(pieces):
        term = jnp.dot(hidden_t[...], ref[...], preferred_element_type=F32)
        terms[:, _at(r, width)] = term.astype(BF16)
    blocks = hidden_t.shape[0] // BLOCK
    _pick_blocks(order_ref, 2, lambda k, j: terms[j, k], outs, blocks)


def _term_blocks(order_ref, weight, normed_t, act_ref, outs, terms):
    terms[...] = jnp.dot(normed_t[...], act_ref[...], preferred_element_type=F32).astype(BF16)
    blocks = terms.shape[1] // BLOCK
    _pick_blocks(order_ref, weight, lambda k, j: terms[k, j], outs, blocks)


def gate_grad_kernel(order_ref, *refs):
    pieces = refs[:8]
    dense, slope_ref, silu_ref, normed_t = refs[8:12]
    outs, up_act = refs[12:16], refs[16]
    grad, gate_act, terms = refs[17:]
    for r, ref in _row_pieces(pieces):
        grad[:, _at(r, ref.shape[1])] = ref[...]
    for n in range(0, up_act.shape[1], TILE):
        cols = slice(n, n + TILE)
        grad_hidden = lax.dot_general(
            grad[...], dense[cols, :], (((1,), (1,)), ((), ())), preferred_element_type=F32
        )
        up_act[:, cols] = (grad_hidden * silu_ref[:, cols]).astype(BF16)
        gate_act[:, cols] = (grad_hidden * slope_ref[:, cols]).astype(BF16)
    _term_blocks(order_ref, 0, normed_t, gate_act, outs, terms)


def up_grad_kernel(order_ref, act_ref, normed_t, *refs):
    _term_blocks(order_ref, 1, normed_t, act_ref, refs[:4], refs[4])


def place_kernel(order_ref, total, gate_out, up_out, down_out):
    col = lax.axis_index("col")
    blocks = gate_out.shape[1] // BLOCK
    for w, out in enumerate((gate_out, up_out, down_out)):
        out[...] = jnp.zeros_like(out)
        for s in range(SLOTS):
            j = order_ref[w * 64 + col * SLOTS + s]

            @pl.when(j < blocks)
            def _(out=out, j=j, w=w, s=s):
                if w == 2:
                    out[_at(j, BLOCK), :] = total[w * SLOTS + s]
                else:
                    out[:, _at(j, BLOCK)] = total[w * SLOTS + s]


def live_order(mask):
    blocks = mask.shape[1]
    i = jnp.arange(blocks, dtype=jnp.int32)
    earlier = (i[None, :] < i[:, None]).astype(jnp.int32)
    place = jnp.sum(mask[:, None, :] * earlier[None], axis=2)
    slot = jnp.where(mask == 1, place, -1)
    hit = slot[:, None, :] == jnp.arange(SLOTS, dtype=jnp.int32)[None, :, None]
    return blocks + jnp.sum(jnp.where(hit, i[None, None, :] - blocks, 0), axis=2)


def row_spread(four):
    return (*four, *(core_swap(v) for v in four))


def per_device(tokens, teacher, gate_weight, up_weight, down_weight, gate_mask, up_mask, down_mask):
    rows, width = tokens.shape
    hidden_n = gate_weight.shape[1]
    full = width * lax.axis_size("row")
    order = live_order(jnp.concatenate([gate_mask, up_mask, down_mask.T], axis=0)).reshape(-1)
    block_shape = lambda *lead: jax.ShapeDtypeStruct((*lead, BLOCK, BLOCK), BF16)

    core = lax.axis_index("row") & 1
    pair = jnp.stack([tokens, core_swap(tokens)])
    near = y_pass(pair)
    half = rows // 2
    far = y_pass(jnp.where(core == 0, near[:, :half], near[:, half:]))
    (live,) = _call(
        pack_kernel, (block_shape(3 * SLOTS),), "pack", 8,
        [pltpu.SMEM(m.shape, m.dtype) for m in (gate_mask, up_mask, down_mask)]
        + [pltpu.VMEM(w.shape, w.dtype) for w in (gate_weight, up_weight, down_weight)]
        + [pltpu.SemaphoreType.DMA((6,))],
        far=range(6),
    )(gate_mask, up_mask, down_mask, gate_weight, up_weight, down_weight)

    lines = gather(live, _plane_shift(0))
    weights = gather(jnp.stack([v[: 2 * SLOTS] for v in lines]), _plane_shift(1))
    line = jnp.stack([v[2 * SLOTS :] for v in lines])
    normed, normed_t = _call(
        norm_kernel,
        (jax.ShapeDtypeStruct((rows, full), BF16), jax.ShapeDtypeStruct((full, rows), BF16)),
        "norm",
        20,
    )(pair, near, core_swap(near), far, core_swap(far))
    line, normed = lax.optimization_barrier((line, normed))
    downs = gather(line, _plane_shift(1))

    act_shape = jax.ShapeDtypeStruct((rows, hidden_n), BF16)
    hidden, slope, silu = _call(
        gate_up_kernel,
        (act_shape,) * 3,
        "gate_up",
        38,
        [
            pltpu.VMEM((2, full, hidden_n + BLOCK), BF16),
            pltpu.VMEM((SIDE, SIDE, 2 * SLOTS, BLOCK, BLOCK), BF16),
            pltpu.VMEM((rows, full), BF16),
            pltpu.VMEM((rows, hidden_n), BF16),
            pltpu.VMEM((rows, hidden_n), BF16),
            pltpu.SemaphoreType.DMA((SIDE + 1,)),
            pltpu.SemaphoreType.DMA((2, hidden_n // TILE)),
        ],
        1,
        far=range(1, 2 + SIDE),
        far_out=(1, 2),
    )(order, normed, *weights)

    part_shape = jax.ShapeDtypeStruct((SIDE, rows, width), BF16)
    part_give, dense_down = _call(
        down_give_kernel,
        (part_shape, jax.ShapeDtypeStruct((hidden_n + BLOCK, full), BF16)),
        "down_give",
        16,
        [
            pltpu.VMEM((SIDE, SIDE, SLOTS, BLOCK, BLOCK), BF16),
            pltpu.SemaphoreType.DMA((SIDE,)),
        ],
        1,
        far=range(2, 2 + SIDE),
    )(order, hidden, *downs)
    (part_keep,) = _call(down_keep_kernel, (part_shape,), "down_keep", 16)(hidden, dense_down)
    (hidden_t,) = _call(
        turn_kernel, (jax.ShapeDtypeStruct((hidden_n, rows), BF16),), "turn", 16
    )(hidden)

    got = core_swap(part_give)
    parts = [part_keep[d].astype(F32) + got[d].astype(F32) for d in range(SIDE)]
    branch = parts[0]
    for v in exchange([p.astype(BF16) for p in parts], y_shift):
        branch = branch + v.astype(F32)
    student = (tokens.astype(F32) + branch).astype(BF16)
    grad_scale = 1.0 / math.sqrt(rows * lax.axis_size("col"))
    grad_tile = ((student.astype(F32) - teacher.astype(F32)) * grad_scale).astype(BF16)
    grads = row_spread(gather(grad_tile, y_shift))

    first, second = _plane_shift(0), _plane_shift(1)
    term_shapes = (block_shape(SIDE, SLOTS),) * SIDE
    down_terms = _call(
        down_grad_kernel,
        term_shapes,
        "down_grad",
        16,
        [pltpu.VMEM((hidden_n, full), BF16)],
        1,
    )(order, hidden_t, *grads)
    *down_terms, normed_t = lax.optimization_barrier((*down_terms, normed_t))
    down_got = exchange(down_terms, first)

    *gate_terms, up_act = _call(
        gate_grad_kernel,
        (*term_shapes, act_shape),
        "gate_grad",
        28,
        [
            pltpu.VMEM((rows, full), BF16),
            pltpu.VMEM((rows, hidden_n), BF16),
            pltpu.VMEM((full, hidden_n), BF16),
        ],
        1,
    )(order, *grads, dense_down, slope, silu, normed_t)
    gate_got = exchange(gate_terms, first)
    up_act, *down_got = lax.optimization_barrier((up_act, *down_got))
    up_terms = _call(
        up_grad_kernel, term_shapes, "up_grad", 24, [pltpu.VMEM((full, hidden_n), BF16)], 1
    )(order, up_act, normed_t)
    up_got = exchange(up_terms, first)

    sums = [
        sum((v.astype(F32) for v in got), own[0].astype(F32))
        for own, got in ((gate_terms, gate_got), (up_terms, up_got), (down_terms, down_got))
    ]
    parts = [jnp.concatenate([v[d] for v in sums]) for d in range(SIDE)]
    total = parts[0]
    for v in exchange([p.astype(BF16) for p in parts], second):
        total = total + v.astype(F32)

    grads_out = [
        jax.ShapeDtypeStruct(w.shape, F32) for w in (gate_weight, up_weight, down_weight)
    ]
    grad_gate, grad_up, grad_down = _call(place_kernel, grads_out, "place", 8, [], 1)(order, total)
    return (student, grad_gate, grad_up, grad_down)


def solution(mesh):
    return jax.shard_map(
        per_device,
        mesh=mesh,
        in_specs=(
            P("col", "row"),
            P("col", "row"),
            P("col", "row"),
            P("col", "row"),
            P("row", "col"),
            P(None, "row"),
            P(None, "row"),
            P("row", None),
        ),
        out_specs=(P("col", "row"), P("col", "row"), P("col", "row"), P("row", "col")),
        check_vma=False,
    )
```

```python
import math

import jax
import jax.numpy as jnp
from jax import lax
from jax.experimental import pallas as pl
from jax.experimental.pallas import tpu as pltpu
from jax.sharding import PartitionSpec as P

BLOCK = 128
EPSILON = 1e-06
SLOTS = 4
SIDE = 4
TILE = 256
BF16 = jnp.bfloat16
F32 = jnp.float32


def _row_perm(dy, flip):
    return [
        (y * 2 + c, ((y + dy) % SIDE) * 2 + (c ^ flip)) for y in range(SIDE) for c in range(2)
    ]


def y_shift(v, d):
    return lax.ppermute(v, "row", _row_perm(d, 0))


def y_pass(v):
    perm = [
        (y * 2 + c, ((y + 1 - 2 * c) % SIDE) * 2 + c) for y in range(SIDE) for c in range(2)
    ]
    return lax.ppermute(v, "row", perm)


def core_swap(v):
    return lax.ppermute(v, "row", _row_perm(0, 1))


def _plane_shift(stage):
    def shift(v, d):
        perm = []
        for y in range(SIDE):
            for c in range(2):
                for x in range(SIDE):
                    for z in range(SIDE):
                        if (c == 0) == (stage == 0):
                            tx, tz = (x + d) % SIDE, z
                        else:
                            tx, tz = x, (z + d) % SIDE
                        r = (y * 2 + c) * 16
                        perm.append((r + x * 4 + z, r + tx * 4 + tz))
        return lax.ppermute(v, ("row", "col"), perm)

    return shift


def gather(v, shift):
    return v, shift(v, -1), shift(v, 2), shift(v, 1)


def exchange(parts, shift):
    return [shift(parts[d], d) for d in range(1, SIDE)]


def _call(kernel, shapes, name, mib, scratch=(), tables=0, far=(), far_out=()):
    def run(*operands):
        smem = pl.BlockSpec(memory_space=pltpu.SMEM)
        vmem = pl.BlockSpec(memory_space=pltpu.VMEM)
        anywhere = pl.BlockSpec(memory_space=pltpu.HBM)
        specs = [smem if n < tables else vmem for n in range(len(operands))]
        return pl.pallas_call(
            kernel,
            out_shape=tuple(
                pltpu.HBM(v.shape, v.dtype) if n in far_out else v for n, v in enumerate(shapes)
            ),
            in_specs=[anywhere if n in far else spec for n, spec in enumerate(specs)],
            out_specs=tuple(anywhere if n in far_out else vmem for n in range(len(shapes))),
            scratch_shapes=list(scratch),
            compiler_params=pltpu.CompilerParams(vmem_limit_bytes=mib << 20),
            name=name,
        )(
            *(
                pltpu.with_memory_space_constraint(v, pltpu.HBM) if n in far else v
                for n, v in enumerate(operands)
            )
        )

    return run


def _at(index, size):
    return pl.ds(pl.multiple_of(index * size, size), size)


def _place():
    row, col = lax.axis_index("row"), lax.axis_index("col")
    return col >> 2, col & 3, row >> 1, row & 1


def _live(bits):
    order = [jnp.int32(-1)] * SLOTS
    seen = jnp.int32(0)
    for j, bit in enumerate(bits):
        for s in range(SLOTS):
            order[s] = jnp.where((bit == 1) & (seen == s), j, order[s])
        seen = seen + bit
    return order


def pack_kernel(*refs):
    sources, out_ref, copies, sems = refs[:6], refs[6], refs[7:13], refs[13]
    loads = [
        pltpu.make_async_copy(src, dst, sems.at[n])
        for n, (src, dst) in enumerate(zip(sources, copies))
    ]
    for load in loads:
        load.start()
    for load in loads:
        load.wait()
    gate_mask, up_mask, down_mask, gate_ref, up_ref, down_ref = copies
    col = lax.axis_index("col")
    count = gate_ref.shape[1] // BLOCK
    gate_live = _live([gate_mask[col, j] for j in range(count)])
    up_live = _live([up_mask[col, j] for j in range(count)])
    down_live = _live([down_mask[j, col] for j in range(count)])

    def block(ref, j, axis):
        at = _at(jnp.maximum(j, 0), BLOCK)
        v = ref[:, at] if axis else ref[at, :]
        return jnp.where(j >= 0, v, jnp.zeros_like(v))

    for s in range(SLOTS):
        out_ref[s] = block(gate_ref, gate_live[s], 1)
        out_ref[SLOTS + s] = block(up_ref, up_live[s], 1)
        out_ref[2 * SLOTS + s] = block(down_ref, down_live[s], 0)


def _row_pieces(refs):
    _, _, y, core = _place()
    for n, ref in enumerate(refs):
        yield ((y + (n & 3)) & 3) * 2 + (core if n < SIDE else 1 - core), ref


def norm_kernel(pair, near, near_swapped, far, far_swapped, out_ref, turned_ref):
    _, _, y, core = _place()
    width, half = pair.shape[2], far.shape[1]
    step = 1 - 2 * core
    for n in range(2):
        mine, theirs = core ^ n, core ^ n ^ 1
        at = lambda dy, c: _at(((y + SIDE + dy) & 3) * 2 + c, width)
        out_ref[:, at(0, mine)] = pair[n]
        out_ref[:, at(-step, mine)] = near[n]
        out_ref[:, at(step, theirs)] = near_swapped[n]
        out_ref[_at(core, half), at(2, mine)] = far[n]
        out_ref[_at(1 - core, half), at(2, theirs)] = far_swapped[n]
    total = None
    for n in range(0, out_ref.shape[1], TILE):
        f = out_ref[:, n : n + TILE].astype(F32)
        total = f * f if total is None else total + f * f
    mean = jnp.sum(total, axis=1, keepdims=True) * (1.0 / out_ref.shape[1])
    scale = lax.rsqrt(mean + EPSILON)
    for n in range(0, out_ref.shape[1], TILE):
        normed = (out_ref[:, n : n + TILE].astype(F32) * scale).astype(BF16)
        out_ref[:, n : n + TILE] = normed
        turned_ref[n : n + TILE, :] = normed.T


def _tile_at(first, second):
    x, z, _, core = _place()
    dx = jnp.where(core == 0, first, second)
    dz = jnp.where(core == 0, second, first)
    return ((x + dx) & 3) * SIDE + ((z + dz) & 3)


def gate_up_kernel(order_ref, x_in, *refs):
    pieces = refs[:SIDE]
    hidden_ref, slope_out, silu_out, *scratch = refs[SIDE:]
    dense, packed, x_ref, slope, silu, in_sems, out_sems = scratch
    loads = [
        pltpu.make_async_copy(pieces[n], packed.at[n], in_sems.at[n]) for n in range(SIDE)
    ]
    loads.append(pltpu.make_async_copy(x_in, x_ref, in_sems.at[SIDE]))
    for load in loads:
        load.start()
    dense[...] = jnp.zeros_like(dense)
    for second in range(SIDE):
        loads[second].wait()
        for first in range(SIDE):
            k = _tile_at(first, second)
            for w in range(2):
                for s in range(SLOTS):
                    j = order_ref[w * 64 + k * SLOTS + s]
                    block = packed[second, first, w * SLOTS + s]
                    dense[w, _at(k, BLOCK), _at(j, BLOCK)] = block
    loads[SIDE].wait()
    stores = []
    for n in range(0, hidden_ref.shape[1], TILE):
        cols = slice(n, n + TILE)
        gate = jnp.dot(x_ref[...], dense[0, :, cols], preferred_element_type=F32)
        up = jnp.dot(x_ref[...], dense[1, :, cols], preferred_element_type=F32)
        sig = jax.nn.sigmoid(gate)
        act = gate * sig
        hidden_ref[:, cols] = (act * up).astype(BF16)
        slope[:, cols] = (up * (sig * (1.0 + gate * (1.0 - sig)))).astype(BF16)
        silu[:, cols] = act.astype(BF16)
        for w, (src, dst) in enumerate(((slope, slope_out), (silu, silu_out))):
            stores.append(
                pltpu.make_async_copy(
                    src.at[:, cols], dst.at[:, cols], out_sems.at[w, n // TILE]
                )
            )
            stores[-1].start()
    for store in stores:
        store.wait()


def _down_part(hidden_ref, dense, out_ref, core):
    y = _place()[2]
    width = out_ref.shape[2]
    for dy in range(SIDE):
        rows = dense[: hidden_ref.shape[1], _at(((y + dy) & 3) * 2 + core, width)]
        out_ref[dy] = jnp.dot(hidden_ref[...], rows, preferred_element_type=F32).astype(BF16)


def down_give_kernel(order_ref, hidden_ref, *refs):
    pieces, (give_ref, dense, packed, sems) = refs[:SIDE], refs[SIDE:]
    loads = [pltpu.make_async_copy(pieces[n], packed.at[n], sems.at[n]) for n in range(SIDE)]
    for load in loads:
        load.start()
    dense[...] = jnp.zeros_like(dense)
    for second in range(SIDE):
        loads[second].wait()
        for first in range(SIDE):
            k = _tile_at(first, second)
            for s in range(SLOTS):
                j = order_ref[128 + k * SLOTS + s]
                dense[_at(j, BLOCK), _at(k, BLOCK)] = packed[second, first, s]
    _down_part(hidden_ref, dense, give_ref, 1 - _place()[3])


def down_keep_kernel(hidden_ref, dense, keep_ref):
    _down_part(hidden_ref, dense, keep_ref, _place()[3])


def turn_kernel(x_ref, out_ref):
    out_ref[...] = x_ref[...].T


def _pick_blocks(order_ref, weight, block_of, outs, blocks):
    for first in range(SIDE):
        for second in range(SIDE):
            k = _tile_at(first, second)
            for s in range(SLOTS):
                j = jnp.minimum(order_ref[weight * 64 + k * SLOTS + s], blocks - 1)
                outs[first][second, s] = block_of(_at(k, BLOCK), _at(j, BLOCK))


def down_grad_kernel(order_ref, hidden_t, *refs):
    pieces, outs, terms = refs[:8], refs[8:12], refs[12]
    width = pieces[0].shape[1]
    for r, ref in _row_pieces(pieces):
        term = jnp.dot(hidden_t[...], ref[...], preferred_element_type=F32)
        terms[:, _at(r, width)] = term.astype(BF16)
    blocks = hidden_t.shape[0] // BLOCK
    _pick_blocks(order_ref, 2, lambda k, j: terms[j, k], outs, blocks)


def _term_blocks(order_ref, weight, normed_t, act_ref, outs, terms):
    terms[...] = jnp.dot(normed_t[...], act_ref[...], preferred_element_type=F32).astype(BF16)
    blocks = terms.shape[1] // BLOCK
    _pick_blocks(order_ref, weight, lambda k, j: terms[k, j], outs, blocks)


def gate_grad_kernel(order_ref, *refs):
    pieces = refs[:8]
    dense, slope_ref, silu_ref, normed_t = refs[8:12]
    outs, up_act = refs[12:16], refs[16]
    grad, gate_act, terms = refs[17:]
    for r, ref in _row_pieces(pieces):
        grad[:, _at(r, ref.shape[1])] = ref[...]
    for n in range(0, up_act.shape[1], TILE):
        cols = slice(n, n + TILE)
        grad_hidden = lax.dot_general(
            grad[...], dense[cols, :], (((1,), (1,)), ((), ())), preferred_element_type=F32
        )
        up_act[:, cols] = (grad_hidden * silu_ref[:, cols]).astype(BF16)
        gate_act[:, cols] = (grad_hidden * slope_ref[:, cols]).astype(BF16)
    _term_blocks(order_ref, 0, normed_t, gate_act, outs, terms)


def up_grad_kernel(order_ref, act_ref, normed_t, *refs):
    _term_blocks(order_ref, 1, normed_t, act_ref, refs[:4], refs[4])


def place_kernel(order_ref, total, gate_out, up_out, down_out):
    col = lax.axis_index("col")
    blocks = gate_out.shape[1] // BLOCK
    for w, out in enumerate((gate_out, up_out, down_out)):
        out[...] = jnp.zeros_like(out)
        for s in range(SLOTS):
            j = order_ref[w * 64 + col * SLOTS + s]

            @pl.when(j < blocks)
            def _(out=out, j=j, w=w, s=s):
                if w == 2:
                    out[_at(j, BLOCK), :] = total[w * SLOTS + s]
                else:
                    out[:, _at(j, BLOCK)] = total[w * SLOTS + s]


def live_order(mask):
    blocks = mask.shape[1]
    i = jnp.arange(blocks, dtype=jnp.int32)
    earlier = (i[None, :] < i[:, None]).astype(jnp.int32)
    place = jnp.sum(mask[:, None, :] * earlier[None], axis=2)
    slot = jnp.where(mask == 1, place, -1)
    hit = slot[:, None, :] == jnp.arange(SLOTS, dtype=jnp.int32)[None, :, None]
    return blocks + jnp.sum(jnp.where(hit, i[None, None, :] - blocks, 0), axis=2)


def row_spread(four):
    return (*four, *(core_swap(v) for v in four))


def per_device(tokens, teacher, gate_weight, up_weight, down_weight, gate_mask, up_mask, down_mask):
    rows, width = tokens.shape
    hidden_n = gate_weight.shape[1]
    full = width * lax.axis_size("row")
    order = live_order(jnp.concatenate([gate_mask, up_mask, down_mask.T], axis=0)).reshape(-1)
    block_shape = lambda *lead: jax.ShapeDtypeStruct((*lead, BLOCK, BLOCK), BF16)

    core = lax.axis_index("row") & 1
    pair = jnp.stack([tokens, core_swap(tokens)])
    near = y_pass(pair)
    half = rows // 2
    far = y_pass(jnp.where(core == 0, near[:, :half], near[:, half:]))
    (live,) = _call(
        pack_kernel, (block_shape(3 * SLOTS),), "pack", 8,
        [pltpu.SMEM(m.shape, m.dtype) for m in (gate_mask, up_mask, down_mask)]
        + [pltpu.VMEM(w.shape, w.dtype) for w in (gate_weight, up_weight, down_weight)]
        + [pltpu.SemaphoreType.DMA((6,))],
        far=range(6),
    )(gate_mask, up_mask, down_mask, gate_weight, up_weight, down_weight)

    lines = gather(live, _plane_shift(0))
    weights = gather(jnp.stack([v[: 2 * SLOTS] for v in lines]), _plane_shift(1))
    line = jnp.stack([v[2 * SLOTS :] for v in lines])
    normed, normed_t = _call(
        norm_kernel,
        (jax.ShapeDtypeStruct((rows, full), BF16), jax.ShapeDtypeStruct((full, rows), BF16)),
        "norm",
        20,
    )(pair, near, core_swap(near), far, core_swap(far))
    weights = list(weights)
    line, normed, weights[2] = lax.optimization_barrier((line, normed, weights[2]))
    downs = gather(line, _plane_shift(1))

    act_shape = jax.ShapeDtypeStruct((rows, hidden_n), BF16)
    hidden, slope, silu = _call(
        gate_up_kernel,
        (act_shape,) * 3,
        "gate_up",
        38,
        [
            pltpu.VMEM((2, full, hidden_n + BLOCK), BF16),
            pltpu.VMEM((SIDE, SIDE, 2 * SLOTS, BLOCK, BLOCK), BF16),
            pltpu.VMEM((rows, full), BF16),
            pltpu.VMEM((rows, hidden_n), BF16),
            pltpu.VMEM((rows, hidden_n), BF16),
            pltpu.SemaphoreType.DMA((SIDE + 1,)),
            pltpu.SemaphoreType.DMA((2, hidden_n // TILE)),
        ],
        1,
        far=range(1, 2 + SIDE),
        far_out=(1, 2),
    )(order, normed, *weights)

    part_shape = jax.ShapeDtypeStruct((SIDE, rows, width), BF16)
    part_give, dense_down = _call(
        down_give_kernel,
        (part_shape, jax.ShapeDtypeStruct((hidden_n + BLOCK, full), BF16)),
        "down_give",
        16,
        [
            pltpu.VMEM((SIDE, SIDE, SLOTS, BLOCK, BLOCK), BF16),
            pltpu.SemaphoreType.DMA((SIDE,)),
        ],
        1,
        far=range(2, 2 + SIDE),
    )(order, hidden, *downs)
    (part_keep,) = _call(down_keep_kernel, (part_shape,), "down_keep", 16)(hidden, dense_down)
    (hidden_t,) = _call(
        turn_kernel, (jax.ShapeDtypeStruct((hidden_n, rows), BF16),), "turn", 16
    )(hidden)

    got = core_swap(part_give)
    parts = [part_keep[d].astype(F32) + got[d].astype(F32) for d in range(SIDE)]
    branch = parts[0]
    for v in exchange([p.astype(BF16) for p in parts], y_shift):
        branch = branch + v.astype(F32)
    student = (tokens.astype(F32) + branch).astype(BF16)
    grad_scale = 1.0 / math.sqrt(rows * lax.axis_size("col"))
    grad_tile = ((student.astype(F32) - teacher.astype(F32)) * grad_scale).astype(BF16)
    grads = row_spread(gather(grad_tile, y_shift))

    first, second = _plane_shift(0), _plane_shift(1)
    term_shapes = (block_shape(SIDE, SLOTS),) * SIDE
    down_terms = _call(
        down_grad_kernel,
        term_shapes,
        "down_grad",
        16,
        [pltpu.VMEM((hidden_n, full), BF16)],
        1,
    )(order, hidden_t, *grads)
    *down_terms, normed_t = lax.optimization_barrier((*down_terms, normed_t))
    down_got = exchange(down_terms, first)

    *gate_terms, up_act = _call(
        gate_grad_kernel,
        (*term_shapes, act_shape),
        "gate_grad",
        28,
        [
            pltpu.VMEM((rows, full), BF16),
            pltpu.VMEM((rows, hidden_n), BF16),
            pltpu.VMEM((full, hidden_n), BF16),
        ],
        1,
    )(order, *grads, dense_down, slope, silu, normed_t)
    gate_got = exchange(gate_terms, first)
    up_act, *down_got = lax.optimization_barrier((up_act, *down_got))
    up_terms = _call(
        up_grad_kernel, term_shapes, "up_grad", 24, [pltpu.VMEM((full, hidden_n), BF16)], 1
    )(order, up_act, normed_t)
    up_got = exchange(up_terms, first)

    sums = [
        sum((v.astype(F32) for v in got), own[0].astype(F32))
        for own, got in ((gate_terms, gate_got), (up_terms, up_got), (down_terms, down_got))
    ]
    parts = [jnp.concatenate([v[d] for v in sums]) for d in range(SIDE)]
    total = parts[0]
    for v in exchange([p.astype(BF16) for p in parts], second):
        total = total + v.astype(F32)

    grads_out = [
        jax.ShapeDtypeStruct(w.shape, F32) for w in (gate_weight, up_weight, down_weight)
    ]
    grad_gate, grad_up, grad_down = _call(place_kernel, grads_out, "place", 8, [], 1)(order, total)
    return (student, grad_gate, grad_up, grad_down)


def solution(mesh):
    return jax.shard_map(
        per_device,
        mesh=mesh,
        in_specs=(
            P("col", "row"),
            P("col", "row"),
            P("col", "row"),
            P("col", "row"),
            P("row", "col"),
            P(None, "row"),
            P(None, "row"),
            P("row", None),
        ),
        out_specs=(P("col", "row"), P("col", "row"), P("col", "row"), P("row", "col")),
        check_vma=False,
    )
```
